128 devices in a mesh: req: 16 (over x, z), kv: 8 (over y, core).
Axes of the slice: x: 4, y: 4, z: 4, core: 2. Of those that a mesh axis runs over, the one named last changes fastest.
Arguments:
- residual_in: bfloat16 [512, 4096], P(None, 'req'), may hold values from -6 to 6
- attn_gain: float32 [4096], replicated, may hold values from 0.1 to 1.9
- query_weight: bfloat16 [4096, 4096], P(None, 'kv'), may hold values from -0.09375 to 0.09375
- key_matrix: bfloat16 [4096, 1024], P(None, 'kv'), may hold values from -0.09375 to 0.09375
- value_matrix: bfloat16 [4096, 1024], P(None, 'kv'), may hold values from -0.09375 to 0.09375
- key_cache: bfloat16 [512, 8, 640, 128], P('req', 'kv'), may hold values from -400 to 400
- cached_values: bfloat16 [512, 8, 640, 128], P('req', 'kv'), may hold values from -6 to 6
- cache_lengths: int32 [512], P('req'), may hold values from 1 to 640, as said below
- positions: int32 [512], P('req'), may hold values from 640 to 16383
- output_weight: bfloat16 [4096, 4096], P(None, 'req'), may hold values from -0.09375 to 0.09375
- mlp_gain: float32 [4096], P('req'), may hold values from 0.1 to 1.9
- gate_weight: bfloat16 [4096, 14336], P('req', 'kv'), may hold values from -0.09375 to 0.09375
- up_weight: bfloat16 [4096, 14336], P('req', 'kv'), may hold values from -0.09375 to 0.09375
- down_weight: bfloat16 [14336, 4096], P('kv', 'req'), may hold values from -0.046875 to 0.046875
Outputs:
- output: bfloat16 [512, 4096], P('kv', 'req')
The draws below stay inside these ranges and needn't reach their ends.
Inputs may be any that keep to these rules, and one draw needn't show every extreme that they name: `cache_lengths`: each request's filled slots; some request has exactly 640 and some exactly 1.
All inputs are finite; a program needn't handle non-finite values.
Results may differ from the reference program's by a relative error of at most 0.025.
Values may be sent and summed in bfloat16 or wider, within the bound.
A program may use at most 128 MiB of HBM per device.

```python
import math
import jax
import jax.numpy as jnp
from jax import lax

MODEL_WIDTH = 4096
FF = 14336
QUERY_HEADS = 32
KEY_VALUE_HEADS = 8
HEAD_WIDTH = 128
CACHE_LENGTH = 640
WINDOW = 512
SINKS = 4
REQ_DEV = 32
REQUEST_TOTAL = 512


def draw_key_cache(key, part):
    array_shape = (REQUEST_TOTAL, KEY_VALUE_HEADS, CACHE_LENGTH, HEAD_WIDTH)
    return jnp.clip(jax.random.normal(key, array_shape, jnp.float32), -6.0, 6.0).astype(jnp.bfloat16)


def draw_cache_lengths(key, part):
    first, second = jax.random.split(jax.random.fold_in(key, 7))
    groups = REQUEST_TOTAL // REQ_DEV
    factor = jax.random.randint(first, (groups,), 1, 5)
    factor = jnp.repeat(factor, REQ_DEV)
    base = jax.random.randint(second, (REQUEST_TOTAL,), 0, CACHE_LENGTH)
    filled = 1 + base * factor // 4
    filled = filled.at[0].set(CACHE_LENGTH)
    filled = filled.at[1].set(1)
    return filled.astype(jnp.int32)


def place_ends(result, key, least, largest):
    place = [jax.random.randint(jax.random.fold_in(key, axis), (), 0, length) for axis, length in enumerate(result.shape)]
    widest = result.shape.index(max(result.shape))
    beside = place[:widest] + [(place[widest] + 1) % result.shape[widest]] + place[widest + 1:]
    return result.at[tuple(place)].set(least).at[tuple(beside)].set(largest)


def steps_of(key, shape, pieces, low, high):
    loudness = 1.0
    for dim, shards_of in pieces:
        steps = jax.random.uniform(jax.random.fold_in(jax.random.fold_in(key, 6), dim), (shards_of,), jnp.float32, low / len(pieces), high / len(pieces))
        loudness = loudness * jnp.repeat(jnp.exp(steps), shape[dim] // shards_of).reshape((-1,) + (1,) * (len(shape) - 1 - dim))
    return loudness


def scatter_about(key, shape, deviation, most, pieces=(), kind=jnp.bfloat16):
    entries = deviation * jax.random.normal(key, shape, jnp.float32)
    if pieces:
        entries = entries * steps_of(key, shape, pieces, -0.22, 0.18)
    return jnp.clip(entries, -most, most).astype(kind)


def setup_inputs(seed: int = 0) -> dict:
    seeds = jax.random.split(jax.random.key(seed), 15)
    residual_in = scatter_about(seeds[0], (REQUEST_TOTAL, MODEL_WIDTH), 1.0, 6.0, ((1, 16),))
    attn_gain = jnp.clip(1.0 + 0.18 * jax.random.normal(seeds[1], (MODEL_WIDTH,), jnp.float32), 0.1, 1.9)
    query_weight = scatter_about(seeds[2], (MODEL_WIDTH, QUERY_HEADS * HEAD_WIDTH), MODEL_WIDTH ** -0.5, 0.09375, ((1, 8),))
    key_matrix = scatter_about(seeds[3], (MODEL_WIDTH, KEY_VALUE_HEADS * HEAD_WIDTH), MODEL_WIDTH ** -0.5, 0.09375, ((1, 8),))
    value_matrix = scatter_about(seeds[4], (MODEL_WIDTH, KEY_VALUE_HEADS * HEAD_WIDTH), MODEL_WIDTH ** -0.5, 0.09375, ((1, 8),))
    key_cache = draw_key_cache(jax.random.fold_in(seeds[14], 71), 0)
    cached_values = scatter_about(seeds[6], (REQUEST_TOTAL, KEY_VALUE_HEADS, CACHE_LENGTH, HEAD_WIDTH), 1.0, 6.0, ((0, 16), (1, 8)))
    cache_lengths = draw_cache_lengths(jax.random.fold_in(seeds[14], 71), 0)
    positions = place_ends(jax.random.randint(seeds[8], (REQUEST_TOTAL,), CACHE_LENGTH, 16384), jax.random.fold_in(seeds[8], 1), CACHE_LENGTH, 16383).astype(jnp.int32)
    output_weight = scatter_about(seeds[9], (QUERY_HEADS * HEAD_WIDTH, MODEL_WIDTH), (QUERY_HEADS * HEAD_WIDTH) ** -0.5, 0.09375, ((1, 16),))
    mlp_gain = jnp.clip(1.0 + 0.18 * jax.random.normal(seeds[10], (MODEL_WIDTH,), jnp.float32), 0.1, 1.9)
    gate_weight = scatter_about(seeds[11], (MODEL_WIDTH, FF), MODEL_WIDTH ** -0.5, 0.09375, ((0, 16), (1, 8)))
    up_weight = scatter_about(seeds[12], (MODEL_WIDTH, FF), MODEL_WIDTH ** -0.5, 0.09375, ((0, 16), (1, 8)))
    down_weight = scatter_about(seeds[13], (FF, MODEL_WIDTH), FF ** -0.5, 0.046875, ((0, 8), (1, 16)))
    return {"residual_in": residual_in, "attn_gain": attn_gain, "query_weight": query_weight, "key_matrix": key_matrix, "value_matrix": value_matrix, "key_cache": key_cache, "cached_values": cached_values, "cache_lengths": cache_lengths, "positions": positions, "output_weight": output_weight, "mlp_gain": mlp_gain, "gate_weight": gate_weight, "up_weight": up_weight, "down_weight": down_weight}


EPS = 1e-05
THETA = 10000.0

def apply_rotary(vectors, places):
    half = vectors.shape[-1] // 2
    freqs = jnp.exp(jnp.arange(half, dtype=jnp.float32) * (-2.0 * math.log(THETA) / vectors.shape[-1]))
    angles = places.astype(jnp.float32)[:, None] * freqs[None, :]
    cosine = jnp.cos(angles)[:, None, :]
    sine = jnp.sin(angles)[:, None, :]
    first = vectors[..., :half]
    second = vectors[..., half:]
    return jnp.concatenate([first * cosine - second * sine, second * cosine + first * sine], axis=-1)

def attend(query_rows, keys, values, new_key, new_value, allowed):
    factor = 1.0 / math.sqrt(query_rows.shape[-1])
    scores = jnp.einsum('bgd,bjd->bgj', query_rows.astype(jnp.float32), keys.astype(jnp.float32)) * factor
    scores = jnp.where(allowed[:, None, :], scores, -1e+30)
    own = jnp.einsum('bgd,bd->bg', query_rows.astype(jnp.float32), new_key.astype(jnp.float32)) * factor
    peak = jnp.maximum(lax.optimization_barrier(jnp.max(scores, axis=-1)), own)
    expo = jnp.where(allowed[:, None, :], jnp.exp(scores - peak[..., None]), 0.0)
    own_expo = jnp.exp(own - peak)
    denom = lax.optimization_barrier(jnp.sum(expo, axis=-1)) + own_expo
    weights = (expo / denom[..., None]).astype(jnp.bfloat16)
    own_weight = (own_expo / denom).astype(jnp.bfloat16)
    mixed = jnp.einsum('bgj,bjd->bgd', weights.astype(jnp.float32), values.astype(jnp.float32))
    mixed = mixed + own_weight.astype(jnp.float32)[..., None] * new_value.astype(jnp.float32)[:, None, :]
    return mixed.astype(jnp.bfloat16)

def reference(residual_in, attn_gain, query_weight, key_matrix, value_matrix, key_cache, cached_values, cache_lengths, positions, output_weight, mlp_gain, gate_weight, up_weight, down_weight):
    slot_count = residual_in.shape[0]
    query_group = QUERY_HEADS // KEY_VALUE_HEADS
    stream = residual_in.astype(jnp.float32)
    normed_input = (stream / jnp.sqrt(lax.optimization_barrier(jnp.sum(stream * stream, axis=-1, keepdims=True)) / MODEL_WIDTH + EPS) * attn_gain).astype(jnp.bfloat16)
    query_rows = jnp.dot(normed_input, query_weight, preferred_element_type=jnp.float32).reshape(slot_count, QUERY_HEADS, HEAD_WIDTH)
    query_rows = apply_rotary(query_rows, positions).astype(jnp.bfloat16).reshape(slot_count, KEY_VALUE_HEADS, query_group, HEAD_WIDTH)
    fresh_keys = jnp.dot(normed_input, key_matrix, preferred_element_type=jnp.float32).reshape(slot_count, KEY_VALUE_HEADS, HEAD_WIDTH)
    fresh_keys = apply_rotary(fresh_keys, positions).astype(jnp.bfloat16)
    fresh_values = jnp.dot(normed_input, value_matrix, preferred_element_type=jnp.float32).reshape(slot_count, KEY_VALUE_HEADS, HEAD_WIDTH).astype(jnp.bfloat16)
    slots = jnp.arange(CACHE_LENGTH, dtype=jnp.int32)[None, :]
    limit = cache_lengths[:, None]
    allowed = (slots < limit) & ((slots < SINKS) | (slots > limit - WINDOW))

    def per_head_rows(head):
        keys = lax.dynamic_index_in_dim(key_cache, head, 1, keepdims=False)
        values = lax.dynamic_index_in_dim(cached_values, head, 1, keepdims=False)
        heads_q = lax.dynamic_index_in_dim(query_rows, head, 1, keepdims=False)
        own_key = lax.dynamic_index_in_dim(fresh_keys, head, 1, keepdims=False)
        own_value = lax.dynamic_index_in_dim(fresh_values, head, 1, keepdims=False)
        return attend(heads_q, keys, values, own_key, own_value, allowed)
    attended_rows = lax.map(per_head_rows, jnp.arange(KEY_VALUE_HEADS, dtype=jnp.int32))
    attended_rows = jnp.transpose(attended_rows, (1, 0, 2, 3)).reshape(slot_count, QUERY_HEADS * HEAD_WIDTH)
    middle = stream + jnp.dot(attended_rows, output_weight, preferred_element_type=jnp.float32)
    scaled = (middle * mlp_gain).astype(jnp.bfloat16)
    inverse = 1.0 / jnp.sqrt(lax.optimization_barrier(jnp.sum(middle * middle, axis=-1, keepdims=True)) / MODEL_WIDTH + EPS)
    gate = jnp.dot(scaled, gate_weight, preferred_element_type=jnp.float32) * inverse
    upper = jnp.dot(scaled, up_weight, preferred_element_type=jnp.float32) * inverse
    hidden = (jax.nn.silu(gate) * upper).astype(jnp.bfloat16)
    return (middle + jnp.dot(hidden, down_weight, preferred_element_type=jnp.float32)).astype(jnp.bfloat16)
```

```python
import functools
import math

import jax
import jax.numpy as jnp
from jax import lax
from jax.experimental import pallas as pl
from jax.experimental.pallas import tpu as pltpu
from jax.sharding import PartitionSpec as P

MODEL_WIDTH = 4096
WINDOW = 512
SINKS = 4
EPS = 1e-05
THETA = 10000.0

NR = 16
NK = 8
ROWS = 32
COLS = 256
FFK = 1792
HEADS = 4
HD = 128
SLOTS = 640
CHUNK = 896

BF = jnp.bfloat16
F32 = jnp.float32
MESH = pl.DeviceIdType.MESH
NT = (((1,), (1,)), ((), ()))
TN = (((0,), (0,)), ((), ()))


def dot(a, b):
    return jnp.dot(a, b, preferred_element_type=F32)


def piece_offset(l):
    return 448 * l + 64 * (l % 2)


def kernel(
    lens, resid, gain1, wq, wk, wv, kc, vc, cosf, sinf, wo, gain2, gw, uw, dw,
    out,
    tok, nrm, wq_v, wk_v, wv_v, k_v, v_v, q3, k3, v3, o3, att, attb, wo_v, res_v,
    gp, up, pk, wp, al, mid, pb, rh, rf, acc1, acc3, hb, dw_v, fs, fb, ownf, sqa, sql, sqm,
    ld, tokS, tokR, wS, wR, attS, attR, b2, yS, alR, lS, al2S, al2R, sqS, sqR, sqlS, sqlR, sqmS, sqmR,
    rhS, rhR, rfS, rfR, hmS, hR, hlS, h2S, h2R, fS, fR,
):
    r = lax.axis_index("req")
    k = lax.axis_index("kv")
    x, z = r // 4, r % 4
    c = k % 2
    l = (1 - c) * x + c * z
    m = (1 - c) * z + c * x

    def dev(li, mi):
        return ((1 - c) * (4 * li + mi) + c * (4 * mi + li), k)

    def rc(src, dst, ss, rs, to):
        return pltpu.make_async_remote_copy(
            src_ref=src, dst_ref=dst, send_sem=ss, recv_sem=rs, device_id=to, device_id_type=MESH
        )

    def arrived(ref, sem):
        pltpu.make_async_copy(ref, ref, sem).wait()

    barrier = pltpu.get_barrier_semaphore()
    for d in range(1, NR):
        pl.semaphore_signal(barrier, inc=1, device_id=((r + d) % NR, k), device_id_type=MESH)
    for d in range(1, NK):
        pl.semaphore_signal(barrier, inc=1, device_id=(r, (k + d) % NK), device_id_type=MESH)

    loads = {}

    def load(name, index, src, dst):
        loads[name] = pltpu.make_async_copy(src, dst, ld.at[index])
        loads[name].start()

    own_tok = pltpu.make_async_copy(resid.at[pl.ds(ROWS * r, ROWS), :], tok.at[r], tokR.at[r])
    own_tok.start()
    load("g3", 0, gw.at[:, pl.ds(384, 128)], gp.at[0])
    load("g10", 1, gw.at[:, pl.ds(1280, 128)], gp.at[1])
    load("u3", 2, uw.at[:, pl.ds(384, 128)], up.at[0])
    load("u10", 3, uw.at[:, pl.ds(1280, 128)], up.at[1])
    load("wq", 4, wq, wq_v)
    load("wk", 5, wk, wk_v)
    load("wv", 6, wv, wv_v)
    load("kc", 7, kc, k_v)
    load("vc", 8, vc, v_v)
    load("wo", 9, wo, wo_v)
    load("res", 10, resid.at[pl.ds(64 * k, 64), :], res_v)
    load("dw", 11, dw, dw_v)

    pl.semaphore_wait(barrier, NR - 1 + NK - 1)
    for d in range(1, NK):
        pl.semaphore_signal(b2, inc=1, device_id=(r, (k + d) % NK), device_id_type=MESH)

    def tok_copy(d):
        to = (r + d) % NR
        return rc(resid.at[pl.ds(ROWS * to, ROWS), :], tok.at[r], tokS.at[d - 1], tokR.at[r], (to, k))

    @pl.loop(1, NR)
    def _(d):
        tok_copy(d).start()

    def w_copies(d):
        to = (l + d) % 4
        off = pl.multiple_of(piece_offset(to), 128)
        pieces = (
            (gw.at[:, pl.ds(off, 384)], wp.at[l, :, pl.ds(0, 384)]),
            (uw.at[:, pl.ds(off, 384)], wp.at[l, :, pl.ds(384, 384)]),
            (pk.at[to], wp.at[l, :, pl.ds(768, 128)]),
        )
        if d == 0:
            return [pltpu.make_async_copy(s, t, wR.at[l]) for s, t in pieces]
        return [rc(s, t, wS.at[3 * (d - 1) + i], wR.at[l], dev(to, m)) for i, (s, t) in enumerate(pieces)]

    w_sends = {d: w_copies(d) for d in range(4)}
    for d in (1, 3, 2, 0):
        w_sends[d][0].start()
        w_sends[d][1].start()
    for name in ("g3", "g10", "u3", "u10"):
        loads[name].wait()
    low = lax.broadcasted_iota(jnp.int32, (COLS, 128), 1) < 64
    for t in range(2):
        g = gp[t].astype(F32)
        u = pltpu.roll(up[t].astype(F32), 64, 1)
        pk[2 * t] = jnp.where(low, g, u).astype(BF)
        pk[2 * t + 1] = jnp.where(low, u, g).astype(BF)
    for d in (1, 3, 2, 0):
        w_sends[d][2].start()

    q3[...] = jnp.zeros_like(q3)
    k3[...] = jnp.zeros_like(k3)
    v3[...] = jnp.zeros_like(v3)

    squares = jnp.zeros((ROWS, COLS), F32)
    for i in range(NR):
        arrived(tok.at[i], tokR.at[i])
    for i in range(NR):
        t = tok[i].astype(F32)
        squares = squares + t * t
    scale = 1.0 / jnp.sqrt(jnp.sum(squares, axis=-1, keepdims=True) / MODEL_WIDTH + EPS)
    for i in range(NR):
        nrm[i] = (tok[i].astype(F32) * scale * gain1[:, COLS * i : COLS * (i + 1)]).astype(BF)
    loads["wq"].wait()
    loads["wk"].wait()
    loads["wv"].wait()
    q = jnp.zeros((ROWS, HEADS * HD), F32)
    kn = jnp.zeros((ROWS, HD), F32)
    vn = jnp.zeros((ROWS, HD), F32)
    for i in range(NR):
        n = nrm[i]
        q = q + dot(n, wq_v[COLS * i : COLS * (i + 1), :])
        kn = kn + dot(n, wk_v[COLS * i : COLS * (i + 1), :])
        vn = vn + dot(n, wv_v[COLS * i : COLS * (i + 1), :])
    cs, sn = cosf[...], sinf[...]

    def rotate(v):
        return (v * cs + pltpu.roll(v, 64, 1) * sn).astype(BF).astype(F32)

    kn = rotate(kn)
    vn = vn.astype(BF).astype(F32)
    for h in range(HEADS):
        q3[pl.ds(h, ROWS, stride=8), :] = rotate(q[:, HD * h : HD * (h + 1)])
        k3[pl.ds(h, ROWS, stride=8), :] = kn
        v3[pl.ds(h, ROWS, stride=8), :] = vn

    loads["kc"].wait()
    loads["vc"].wait()
    factor = 1.0 / math.sqrt(HD)
    slot = lax.broadcasted_iota(jnp.int32, (8, SLOTS), 1)

    def attend(b):
        rows = pl.ds(pl.multiple_of(8 * b, 8), 8)
        qb = q3[rows, :]
        s = lax.dot_general(qb.astype(BF), k_v[b], NT, preferred_element_type=F32) * factor
        n = lens[b]
        ok = (slot < n) & ((slot < SINKS) | (slot > n - WINDOW))
        s = jnp.where(ok, s, -1e30)
        own = jnp.sum(qb * k3[rows, :], axis=-1, keepdims=True) * factor
        peak = jnp.maximum(jnp.max(s, axis=-1, keepdims=True), own)
        e = jnp.where(ok, jnp.exp(s - peak), 0.0)
        eo = jnp.exp(own - peak)
        inv = 1.0 / (jnp.sum(e, axis=-1, keepdims=True) + eo)
        w = (e * inv).astype(BF)
        wo_ = (eo * inv).astype(BF).astype(F32)
        o3[rows, :] = dot(w, v_v[b]) + wo_ * v3[rows, :]

    kd = r // 2

    def att_copy(half, d):
        to = (r + d) % NR
        rows = pl.ds(16 * half, 16)
        there = pl.ds(pl.multiple_of((r % 2) * 32 + 16 * half, 16), 16)
        return (att.at[rows, :], attb.at[k, there, :], attS.at[16 * half + d], attR.at[k, r % 2], (to, kd))

    for half in range(2):

        @pl.loop(0, 4)
        def _(g):
            for j in range(4):
                attend(16 * half + 4 * g + j)

        for h in range(HEADS):
            att[16 * half : 16 * half + 16, HD * h : HD * (h + 1)] = o3[
                pl.ds(128 * half + h, 16, stride=8), :
            ].astype(BF)
        if half == 0:
            pl.semaphore_wait(b2, NK - 1)

        @pl.when(k == kd)
        def _():
            src, dst, _, rs, _ = att_copy(half, 0)
            pltpu.make_async_copy(src, dst, rs).start()

        @pl.when(k != kd)
        def _():
            rc(*att_copy(half, 0)).start()

        @pl.loop(1, NR)
        def _(d):
            rc(*att_copy(half, d)).start()

    loads["wo"].wait()
    loads["res"].wait()
    for i in range(NK):
        for p in range(2):
            arrived(attb.at[i, pl.ds(32 * p, 32), :], attR.at[i, p])
    o = res_v[...].astype(F32)
    for i in range(NK):
        o = o + dot(attb[i], wo_v[512 * i : 512 * (i + 1), :])
    mid[...] = o
    blk = pl.ds(pl.multiple_of(64 * k, 64), 64)
    al[l, blk, :] = (o * gain2[...]).astype(BF)
    o2 = jnp.concatenate([o * o, jnp.zeros_like(o)], axis=0)
    sqa[k] = lax.dot_general(
        jnp.ones((8, COLS), F32), o2, NT, preferred_element_type=F32, precision=lax.Precision.HIGHEST
    )

    ends = []

    def go(copy):
        copy.start()
        ends.append(copy)

    order = (1, 7, 2, 6, 3, 5, 4)
    for i, d in enumerate(order):
        kp = (k + d) % NK
        cp = kp % 2
        lp = (1 - cp) * x + cp * z
        go(rc(al.at[l, blk, :], al.at[lp, blk, :], yS.at[i], alR.at[lp, k], (r, kp)))
        go(rc(sqa.at[k], sqa.at[k], sqS.at[i], sqR.at[k], (r, kp)))
    nxt, prv = (l + 1) % 4, (l + 3) % 4
    for i, d in enumerate((0,) + order):
        kp = (k + d) % NK
        at = pl.ds(pl.multiple_of(64 * kp, 64), 64)
        if d:
            arrived(al.at[l, at, :], alR.at[l, kp])
        go(rc(al.at[l, at, :], al.at[l, at, :], lS.at[0, i], alR.at[l, kp], dev(nxt, m)))
        go(rc(al.at[l, at, :], al.at[l, at, :], lS.at[1, i], alR.at[l, kp], dev(prv, m)))
    for d in order:
        kp = (k + d) % NK
        arrived(sqa.at[kp], sqR.at[kp])
    sub = lax.broadcasted_iota(jnp.int32, (8, 128), 0)
    t = jnp.zeros((8, 128), F32)
    for i in range(NK):
        t = t + jnp.where(sub == i, sqa[i], 0.0)
    sql[l] = t
    for d in range(1, 4):
        go(rc(sql.at[l], sql.at[l], sqlS.at[d - 1], sqlR.at[l], dev((l + d) % 4, m)))
    for i, d in enumerate((0,) + order):
        kp = (k + d) % NK
        at = pl.ds(pl.multiple_of(64 * kp, 64), 64)
        first = pl.ds(pl.multiple_of(64 * kp, 32), 32)
        second = pl.ds(pl.multiple_of(64 * kp + 32, 32), 32)
        arrived(al.at[prv, at, :], alR.at[prv, kp])
        go(rc(al.at[prv, first, :], al.at[prv, first, :], al2S.at[0, i], al2R.at[0, kp], dev(nxt, m)))
        arrived(al.at[nxt, at, :], alR.at[nxt, kp])
        go(rc(al.at[nxt, second, :], al.at[nxt, second, :], al2S.at[1, i], al2R.at[1, kp], dev(prv, m)))
    for d in range(1, 4):
        at = (l + d) % 4
        arrived(sql.at[at], sqlR.at[at])
    sqm[m] = sql[0] + sql[1] + sql[2] + sql[3]
    for d in range(1, 4):
        go(rc(sqm.at[m], sqm.at[m], sqmS.at[d - 1], sqmR.at[m], dev(l, (m + d) % 4)))
    far = (l + 2) % 4
    for i, d in enumerate((0,) + order):
        kp = (k + d) % NK
        arrived(al.at[far, pl.ds(pl.multiple_of(64 * kp, 32), 32), :], al2R.at[0, kp])
        arrived(al.at[far, pl.ds(pl.multiple_of(64 * kp + 32, 32), 32), :], al2R.at[1, kp])
    for i in range(4):
        arrived(wp.at[i], wR.at[i])

    def part(mi):
        rows = pl.ds(pl.multiple_of(128 * mi, 128), 128)
        total = dot(al[0, rows, :], wp[0])
        for i in range(1, 4):
            total = total + dot(al[i, rows, :], wp[i])
        return total

    m1, m2, m3 = (m + 1) % 4, (m + 2) % 4, (m + 3) % 4
    pb[2] = part(m2).astype(BF)
    go(rc(pb.at[2, pl.ds(0, 64), :], rh.at[0], rhS.at[0], rhR.at[0], dev(l, m1)))
    go(rc(pb.at[2, pl.ds(64, 64), :], rh.at[1], rhS.at[1], rhR.at[1], dev(l, m3)))
    acc1[...] = part(m1)
    acc3[...] = part(m3)
    arrived(rh.at[0], rhR.at[0])
    pb[0, 0:64, :] = (acc1[0:64, :] + rh[0].astype(F32)).astype(BF)
    pb[0, 64:128, :] = acc1[64:128, :].astype(BF)
    go(rc(pb.at[0], rf.at[0], rfS.at[0], rfR.at[0], dev(l, m1)))
    arrived(rh.at[1], rhR.at[1])
    pb[1, 0:64, :] = acc3[0:64, :].astype(BF)
    pb[1, 64:128, :] = (acc3[64:128, :] + rh[1].astype(F32)).astype(BF)
    go(rc(pb.at[1], rf.at[1], rfS.at[1], rfR.at[1], dev(l, m3)))
    acc1[...] = part(m)
    for d in range(1, 4):
        at = (m + d) % 4
        arrived(sqm.at[at], sqmR.at[at])
    sq = sqm[0] + sqm[1] + sqm[2] + sqm[3]
    pick = [
        lax.dot_general(
            sq,
            (sub == 2 * m + i).astype(F32),
            TN,
            preferred_element_type=F32,
            precision=lax.Precision.HIGHEST,
        )[0:64, :]
        for i in range(2)
    ]
    inv = 1.0 / jnp.sqrt(jnp.concatenate(pick, axis=0) / MODEL_WIDTH + EPS)
    arrived(rf.at[0], rfR.at[0])
    arrived(rf.at[1], rfR.at[1])
    mine = pl.ds(pl.multiple_of(128 * m, 128), 128)

    def tile(i):
        at = slice(128 * i, 128 * (i + 1))
        return (acc1[:, at] + rf[0, :, at].astype(F32) + rf[1, :, at].astype(F32)) * inv

    def silu(v):
        return v / (1.0 + jnp.exp(-v))

    for i in range(3):
        hb[l, mine, 128 * i : 128 * (i + 1)] = (silu(tile(i)) * tile(3 + i)).astype(BF)
    t = tile(6)
    lane = lax.broadcasted_iota(jnp.int32, (128, 128), 1)
    hb[l, mine, 384:512] = jnp.where(lane // 64 == l % 2, silu(t) * pltpu.roll(t, 64, 1), 0.0).astype(BF)

    for i, d in enumerate((1, 3, 2)):
        go(rc(hb.at[l, mine, :], hb.at[l, mine, :], hmS.at[i], hR.at[l, m], dev(l, (m + d) % 4)))
    for i, d in enumerate((0, 1, 3, 2)):
        mi = (m + d) % 4
        at = pl.ds(pl.multiple_of(128 * mi, 128), 128)
        if d:
            arrived(hb.at[l, at, :], hR.at[l, mi])
        go(rc(hb.at[l, at, :], hb.at[l, at, :], hlS.at[0, i], hR.at[l, mi], dev(nxt, m)))
        go(rc(hb.at[l, at, :], hb.at[l, at, :], hlS.at[1, i], hR.at[l, mi], dev(prv, m)))
    for i, d in enumerate((0, 1, 3, 2)):
        mi = (m + d) % 4
        at = pl.ds(pl.multiple_of(128 * mi, 128), 128)
        first = pl.ds(pl.multiple_of(128 * mi, 64), 64)
        second = pl.ds(pl.multiple_of(128 * mi + 64, 64), 64)
        arrived(hb.at[prv, at, :], hR.at[prv, mi])
        go(rc(hb.at[prv, first, :], hb.at[prv, first, :], h2S.at[0, i], h2R.at[0, mi], dev(nxt, m)))
        arrived(hb.at[nxt, at, :], hR.at[nxt, mi])
        go(rc(hb.at[nxt, second, :], hb.at[nxt, second, :], h2S.at[1, i], h2R.at[1, mi], dev(prv, m)))

    loads["dw"].wait()

    def last_copy(kp):
        return rc(fs.at[kp], fb.at[k], fS.at[kp], fR.at[k], (r, kp))

    for d in (0, 1, 3, 2):
        mi = (m + d) % 4
        at = pl.ds(pl.multiple_of(128 * mi, 128), 128)
        arrived(hb.at[far, pl.ds(pl.multiple_of(128 * mi, 64), 64), :], h2R.at[0, mi])
        arrived(hb.at[far, pl.ds(pl.multiple_of(128 * mi + 64, 64), 64), :], h2R.at[1, mi])
        y = dot(hb[0, at, 0:384], dw_v[0:384, :])
        for i in range(1, 4):
            off = piece_offset(i)
            y = y + dot(hb[i, at, 0:384], dw_v[off : off + 384, :])
        for i in range(2):
            off = 384 + 896 * i
            y = y + dot(hb[2 * i, at, 384:512] + hb[2 * i + 1, at, 384:512], dw_v[off : off + 128, :])
        for i in range(2):
            kp = 2 * mi + i
            fs[kp] = y[64 * i : 64 * (i + 1), :].astype(BF)

            @pl.when(kp == k)
            def _():
                ownf[...] = y[64 * i : 64 * (i + 1), :]

            @pl.when(kp != k)
            def _():
                last_copy(kp).start()

    total = mid[...] + ownf[...]
    for d in range(1, NK):
        kp = (k + d) % NK
        arrived(fb.at[kp], fR.at[kp])
        total = total + fb[kp].astype(F32)
    out[...] = total.astype(BF)

    @pl.loop(1, NR)
    def _(d):
        tok_copy(d).wait_send()

    for d in range(1, 4):
        for copy in w_sends[d]:
            copy.wait_send()
    for half in range(2):

        @pl.when(k != kd)
        def _():
            rc(*att_copy(half, 0)).wait_send()

        @pl.loop(1, NR)
        def _(d):
            rc(*att_copy(half, d)).wait_send()

    for copy in ends:
        copy.wait_send()
    for d in range(1, NK):
        last_copy((k + d) % NK).wait_send()


def shards(
    residual_in,
    attn_gain,
    query_weight,
    key_matrix,
    value_matrix,
    key_cache,
    cached_values,
    cache_lengths,
    positions,
    output_weight,
    mlp_gain,
    gate_weight,
    up_weight,
    down_weight,
):
    half = HD // 2
    freqs = jnp.exp(jnp.arange(half, dtype=F32) * (-2.0 * math.log(THETA) / HD))
    angles = positions.astype(F32)[:, None] * freqs[None, :]
    cosine, sine = jnp.cos(angles), jnp.sin(angles)
    cosf = jnp.concatenate([cosine, cosine], axis=-1)
    sinf = jnp.concatenate([-sine, sine], axis=-1)
    hbm = pl.BlockSpec(memory_space=pltpu.MemorySpace.HBM)
    vmem = pl.BlockSpec(memory_space=pltpu.MemorySpace.VMEM)
    smem = pl.BlockSpec(memory_space=pltpu.MemorySpace.SMEM)
    V = pltpu.VMEM
    dma = lambda *shape: pltpu.SemaphoreType.DMA(shape)
    return pl.pallas_call(
        kernel,
        out_shape=jax.ShapeDtypeStruct((64, COLS), BF),
        in_specs=[smem, hbm, vmem, hbm, hbm, hbm, hbm, hbm, vmem, vmem, hbm, vmem, hbm, hbm, hbm],
        out_specs=vmem,
        scratch_shapes=[
            V((NR, ROWS, COLS), BF),
            V((NR, ROWS, COLS), BF),
            V((MODEL_WIDTH, HEADS * HD), BF),
            V((MODEL_WIDTH, HD), BF),
            V((MODEL_WIDTH, HD), BF),
            V((ROWS, SLOTS, HD), BF),
            V((ROWS, SLOTS, HD), BF),
            V((8 * ROWS, HD), F32),
            V((8 * ROWS, HD), F32),
            V((8 * ROWS, HD), F32),
            V((8 * ROWS, HD), F32),
            V((ROWS, HEADS * HD), BF),
            V((NK, 64, HEADS * HD), BF),
            V((MODEL_WIDTH, COLS), BF),
            V((64, COLS), BF),
            V((2, COLS, 128), BF),
            V((2, COLS, 128), BF),
            V((4, COLS, 128), BF),
            V((4, COLS, CHUNK), BF),
            V((4, 512, COLS), BF),
            V((64, COLS), F32),
            V((3, 128, CHUNK), BF),
            V((2, 64, CHUNK), BF),
            V((2, 128, CHUNK), BF),
            V((128, CHUNK), F32),
            V((128, CHUNK), F32),
            V((4, 512, 512), BF),
            V((FFK, COLS), BF),
            V((NK, 64, COLS), BF),
            V((NK, 64, COLS), BF),
            V((64, COLS), F32),
            V((NK, 8, 128), F32),
            V((4, 8, 128), F32),
            V((4, 8, 128), F32),
            dma(12),
            dma(NR - 1),
            dma(NR),
            dma(9),
            dma(4),
            dma(32),
            dma(NK, 2),
            pltpu.SemaphoreType.REGULAR,
            dma(NK - 1),
            dma(4, NK),
            dma(2, NK),
            dma(2, NK),
            dma(2, NK),
            dma(NK - 1),
            dma(NK),
            dma(3),
            dma(4),
            dma(3),
            dma(4),
            dma(2),
            dma(2),
            dma(2),
            dma(2),
            dma(3),
            dma(4, 4),
            dma(2, 4),
            dma(2, 4),
            dma(2, 4),
            dma(NK),
            dma(NK),
        ],
        compiler_params=pltpu.CompilerParams(
            collective_id=0, has_side_effects=True, vmem_limit_bytes=56 << 20
        ),
    )(
        cache_lengths,
        residual_in,
        attn_gain.reshape(1, MODEL_WIDTH),
        query_weight,
        key_matrix,
        value_matrix,
        key_cache.reshape(ROWS, SLOTS, HD),
        cached_values.reshape(ROWS, SLOTS, HD),
        cosf,
        sinf,
        output_weight,
        mlp_gain.reshape(1, COLS),
        gate_weight,
        up_weight,
        down_weight,
    )


def solution(mesh):
    return jax.shard_map(
        shards,
        mesh=mesh,
        in_specs=(
            P(None, "req"),
            P(),
            P(None, "kv"),
            P(None, "kv"),
            P(None, "kv"),
            P("req", "kv", None, None),
            P("req", "kv", None, None),
            P("req"),
            P("req"),
            P(None, "req"),
            P("req"),
            P("req", "kv"),
            P("req", "kv"),
            P("kv", "req"),
        ),
        out_specs=P("kv", "req"),
        check_vma=False,
    )
```

```python
import functools
import math

import jax
import jax.numpy as jnp
from jax import lax
from jax.experimental import pallas as pl
from jax.experimental.pallas import tpu as pltpu
from jax.sharding import PartitionSpec as P

MODEL_WIDTH = 4096
WINDOW = 512
SINKS = 4
EPS = 1e-05
THETA = 10000.0

NR = 16
NK = 8
ROWS = 32
COLS = 256
FFK = 1792
HEADS = 4
HD = 128
SLOTS = 640
CHUNK = 896

BF = jnp.bfloat16
F32 = jnp.float32
MESH = pl.DeviceIdType.MESH
NT = (((1,), (1,)), ((), ()))
TN = (((0,), (0,)), ((), ()))


def dot(a, b):
    return jnp.dot(a, b, preferred_element_type=F32)


def piece_offset(l):
    return 448 * l + 64 * (l % 2)


def kernel(
    lens, pos, resid, gain1, wq, wk, wv, kc, vc, wo, gain2, gw, uw, dw,
    out,
    tok, nrm, wq_v, wk_v, wv_v, k_v, v_v, q3, k3, v3, o3, s3, w3, att, attb, wo_v, res_v,
    gp, up, pk, wp, dwp, gl, al, mid, pb, rf, acc, hb, yb, yr, yown, fs, fb, ownf, sqs, sqm,
    ld, tokS, tokR, wS, wR, dS, dR, gS, gR, attS, attR, b2, yS, yR, lS, alR, sqS, sqR,
    rfS, rfR, hS, hR, oS, oR, fS, fR,
):
    r = lax.axis_index("req")
    k = lax.axis_index("kv")
    x, z = r // 4, r % 4
    y, c = k // 2, k % 2
    l = (1 - c) * x + c * z
    m = (1 - c) * z + c * x

    def dev(li, mi):
        return ((1 - c) * (4 * li + mi) + c * (4 * mi + li), k)

    def rc(src, dst, ss, rs, to):
        return pltpu.make_async_remote_copy(
            src_ref=src, dst_ref=dst, send_sem=ss, recv_sem=rs, device_id=to, device_id_type=MESH
        )

    def arrived(ref, sem):
        pltpu.make_async_copy(ref, ref, sem).wait()

    def rows_of(i, n):
        return pl.ds(pl.multiple_of(n * i, n), n)

    barrier = pltpu.get_barrier_semaphore()
    for d in range(1, NR):
        pl.semaphore_signal(barrier, inc=1, device_id=((r + d) % NR, k), device_id_type=MESH)
    for d in range(1, NK):
        pl.semaphore_signal(barrier, inc=1, device_id=(r, (k + d) % NK), device_id_type=MESH)

    loads = {}

    def load(name, src, dst):
        loads[name] = pltpu.make_async_copy(src, dst, ld.at[len(loads)])
        loads[name].start()

    pltpu.make_async_copy(resid.at[rows_of(r, ROWS), :], tok.at[:, rows_of(r, COLS)], tokR).start()
    load("g3", gw.at[:, pl.ds(384, 128)], gp.at[0])
    load("g10", gw.at[:, pl.ds(1280, 128)], gp.at[1])
    load("u3", uw.at[:, pl.ds(384, 128)], up.at[0])
    load("u10", uw.at[:, pl.ds(1280, 128)], up.at[1])
    load("wq", wq, wq_v)
    load("wk", wk, wk_v)
    load("wv", wv, wv_v)
    load("kc", kc, k_v)
    load("vc", vc, v_v)
    load("wo", wo, wo_v)
    load("res", resid.at[rows_of(k, 64), :], res_v)

    pl.semaphore_wait(barrier, NR - 1 + NK - 1)

    for d in range(1, NR):
        to = (r + d) % NR
        rc(resid.at[rows_of(to, ROWS), :], tok.at[:, rows_of(r, COLS)], tokS, tokR, (to, k)).start()
    for d in range(1, NK):
        pl.semaphore_signal(b2, inc=1, device_id=(r, (k + d) % NK), device_id_type=MESH)

    def w_copies(d):
        to = (l + d) % 4
        off = pl.multiple_of(piece_offset(to), 128)
        here = rows_of(l, COLS)
        pieces = (
            (gw.at[:, pl.ds(off, 384)], wp.at[here, pl.ds(0, 384)]),
            (uw.at[:, pl.ds(off, 384)], wp.at[here, pl.ds(384, 384)]),
            (pk.at[to], wp.at[here, pl.ds(768, 128)]),
        )
        if d == 0:
            return [pltpu.make_async_copy(s, t, wR) for s, t in pieces]
        return [rc(s, t, wS, wR, dev(to, m)) for s, t in pieces]

    def d_copies(d):
        to = (l + d) % 4
        off = pl.multiple_of(piece_offset(to), 64)
        off2 = pl.multiple_of(384 + 896 * (to // 2) + 64 * (to % 2), 64)
        here = rows_of(l, COLS)
        pieces = (
            (dw.at[pl.ds(off, 384), :], dwp.at[pl.ds(0, 384), here]),
            (dw.at[pl.ds(off2, 64), :], dwp.at[pl.ds(384, 64), here]),
        )
        if d == 0:
            return [pltpu.make_async_copy(s, t, dR) for s, t in pieces]
        return [rc(s, t, dS, dR, dev(to, m)) for s, t in pieces]

    w_sends = {d: w_copies(d) for d in range(4)}
    for d in (1, 3, 2, 0):
        w_sends[d][0].start()
        w_sends[d][1].start()
    for name in ("g3", "g10", "u3", "u10"):
        loads[name].wait()
    low = lax.broadcasted_iota(jnp.int32, (COLS, 128), 1) < 64
    for t in range(2):
        g = gp[t].astype(F32)
        u = up[t].astype(F32)
        pk[2 * t] = jnp.where(low, g, pltpu.roll(u, 64, 1)).astype(BF)
        pk[2 * t + 1] = jnp.where(low, pltpu.roll(g, 64, 1), u).astype(BF)
    for d in (1, 3, 2, 0):
        w_sends[d][2].start()
    gl[l] = gain2[...]
    for d in range(1, 4):
        rc(gain2, gl.at[l], gS.at[d - 1], gR.at[l], dev((l + d) % 4, m)).start()
    for d in (1, 3, 2, 0):
        for copy in d_copies(d):
            copy.start()

    q3[...] = jnp.zeros_like(q3)
    k3[...] = jnp.zeros_like(k3)
    v3[...] = jnp.zeros_like(v3)
    dwp[448:512, :] = jnp.zeros((64, 1024), BF)

    sub = lax.broadcasted_iota(jnp.int32, (8, 128), 0)
    lane = lax.broadcasted_iota(jnp.int32, (ROWS, HD), 1)
    p8 = jnp.broadcast_to(pos[...].astype(F32), (8, ROWS))
    place = lax.dot_general(
        p8, (sub == 0).astype(F32), TN, preferred_element_type=F32, precision=lax.Precision.HIGHEST
    )
    freq = jnp.exp((lane % 64).astype(F32) * (-2.0 * math.log(THETA) / HD))
    angle = place * freq
    cs = jnp.cos(angle)
    sn = jnp.where(lane < 64, -1.0, 1.0) * jnp.sin(angle)

    arrived(tok, tokR)
    t = tok[...].astype(F32)
    scale = 1.0 / jnp.sqrt(jnp.sum(t * t, axis=-1, keepdims=True) / MODEL_WIDTH + EPS)
    nrm[...] = (t * scale * gain1[...]).astype(BF)
    loads["wq"].wait()
    loads["wk"].wait()
    loads["wv"].wait()
    q = dot(nrm[...], wq_v[...])
    kn = dot(nrm[...], wk_v[...])
    vn = dot(nrm[...], wv_v[...])

    def rotate(v):
        return (v * cs + pltpu.roll(v, 64, 1) * sn).astype(BF).astype(F32)

    kn = rotate(kn)
    vn = vn.astype(BF).astype(F32)
    for h in range(HEADS):
        q3[pl.ds(h, ROWS, stride=8), :] = rotate(q[:, HD * h : HD * (h + 1)])
        k3[pl.ds(h, ROWS, stride=8), :] = kn
        v3[pl.ds(h, ROWS, stride=8), :] = vn

    factor = 1.0 / math.sqrt(HD)
    slot = lax.broadcasted_iota(jnp.int32, (8, SLOTS), 1)
    loads["kc"].wait()
    for half in range(2):
        for b in range(16 * half, 16 * half + 16):
            rows = slice(8 * b, 8 * b + 8)
            s = lax.dot_general(q3[rows, :].astype(BF), k_v[b], NT, preferred_element_type=F32)
            n = lens[b]
            ok = (slot < n) & ((slot < SINKS) | (slot > n - WINDOW))
            s3[rows, :] = jnp.where(ok, s * factor, -1e30)
        rows = slice(128 * half, 128 * half + 128)
        s = s3[rows, :]
        own = jnp.sum(q3[rows, :] * k3[rows, :], axis=-1, keepdims=True) * factor
        peak = jnp.maximum(jnp.max(s, axis=-1, keepdims=True), own)
        e = jnp.where(s > -1e29, jnp.exp(s - peak), 0.0)
        eo = jnp.exp(own - peak)
        inv = 1.0 / (jnp.sum(e, axis=-1, keepdims=True) + eo)
        w3[rows, :] = e * inv
        o3[rows, :] = (eo * inv).astype(BF).astype(F32) * v3[rows, :]
        if half == 0:
            loads["vc"].wait()
        for b in range(16 * half, 16 * half + 16):
            rows = slice(8 * b, 8 * b + 8)
            o3[rows, :] += dot(w3[rows, :].astype(BF), v_v[b])
    for h in range(HEADS):
        att[:, HD * h : HD * (h + 1)] = o3[pl.ds(h, ROWS, stride=8), :].astype(BF)

    kd = r // 2
    there = attb.at[rows_of(r % 2, ROWS), rows_of(k, 512)]
    pl.semaphore_wait(b2, NK - 1)

    @pl.when(k == kd)
    def _():
        pltpu.make_async_copy(att, there, attR).start()

    @pl.when(k != kd)
    def _():
        rc(att, there, attS, attR, (r, kd)).start()

    for d in range(1, NR):
        rc(att, there, attS, attR, ((r + d) % NR, kd)).start()

    arrived(tok.at[:, pl.ds(0, COLS * 15)], tokS)
    arrived(wp.at[pl.ds(0, 768), :], wS)
    for d in range(1, 4):
        rc(gain2, gl.at[l], gS.at[d - 1], gR.at[l], dev((l + d) % 4, m)).wait_send()
    arrived(dwp.at[pl.ds(0, 448), pl.ds(0, 768)], dS)

    loads["wo"].wait()
    loads["res"].wait()
    arrived(attb, attR)
    o = res_v[...].astype(F32) + dot(attb[...], wo_v[...])
    mid[...] = o
    blk = rows_of(k, 64)
    al[blk, rows_of(l, COLS)] = (o * gain2[...]).astype(BF)

    def peer(d):
        return 2 * ((y + d // 2) % 4) + (c + d % 2) % 2

    for i, d in enumerate((1, 2, 3, 6, 7, 4, 5)):
        kp = peer(d)
        cp = kp % 2
        lp = (1 - cp) * x + cp * z
        rc(al.at[blk, rows_of(l, COLS)], al.at[blk, rows_of(lp, COLS)], yS, yR.at[k], (r, kp)).start()
    mycols = rows_of(l, COLS)

    @pl.when(k == kd)
    def _():
        arrived(attb.at[pl.ds(0, 32), pl.ds(0, 3584)], attS)
        arrived(attb.at[pl.ds(32, 32), pl.ds(0, 4096)], attS)

    @pl.when(k != kd)
    def _():
        arrived(attb, attS)

    for i, d in enumerate((0, 1, 3, 2)):
        yp = (y + d) % 4
        for h in range(2):
            kp = 2 * yp + (c + h) % 2
            if d or h:
                arrived(al.at[rows_of(kp, 64), mycols], yR.at[kp])
        at = rows_of(yp, 128)
        for e in (1, 3, 2):
            rc(al.at[at, mycols], al.at[at, mycols], lS, alR.at[l, yp], dev((l + e) % 4, m)).start()

    arrived(wp, wR)
    for d in range(1, 4):
        at = (l + d) % 4
        arrived(gl.at[at], gR.at[at])
    ginv = [1.0 / gl[i] for i in range(4)]
    for i, d in enumerate((0, 1, 3, 2)):
        mi = (y + d) % 4
        at = rows_of(mi, 128)
        for e in (1, 3, 2):
            lp = (l + e) % 4
            arrived(al.at[at, rows_of(lp, COLS)], alR.at[lp, mi])
        p = dot(al[at, :], wp[...])
        part = jnp.zeros((128, 128), F32)
        for j in range(8):
            g = ginv[j // 2][:, 128 * (j % 2) : 128 * (j % 2) + 128]
            v = al[at, 128 * j : 128 * (j + 1)].astype(F32) * g
            part = part + v * v
        sqs[i] = lax.dot_general(
            jnp.ones((8, 128), F32), part, NT, preferred_element_type=F32, precision=lax.Precision.HIGHEST
        )

        @pl.when(mi == m)
        def _():
            acc[...] = p
            sqm[m] = sqs[i]

        @pl.when(mi != m)
        def _():
            pb[i] = p.astype(BF)
            rc(pb.at[i], rf.at[m], rfS.at[i], rfR.at[m], dev(l, mi)).start()
            rc(sqs.at[i], sqm.at[m], sqS.at[i], sqR.at[m], dev(l, mi)).start()

    arrived(al.at[pl.ds(0, 448), pl.ds(0, COLS)], yS)
    arrived(al.at[:, pl.ds(0, 768)], lS)

    for d in (1, 3, 2):
        at = (m + d) % 4
        arrived(sqm.at[at], sqR.at[at])
    sq = sqm[0] + sqm[1] + sqm[2] + sqm[3]
    total = lax.dot_general(
        sq, (sub == 0).astype(F32), TN, preferred_element_type=F32, precision=lax.Precision.HIGHEST
    )
    inv = 1.0 / jnp.sqrt(total / MODEL_WIDTH + EPS)
    for d in (1, 3, 2):
        at = (m + d) % 4
        arrived(rf.at[at], rfR.at[at])
        acc[...] += rf[at].astype(F32)
    mine = rows_of(m, 128)

    def tile(i):
        return acc[:, 128 * i : 128 * (i + 1)] * inv

    def silu(v):
        return v / (1.0 + jnp.exp(-v))

    for i in range(3):
        hb[mine, 128 * i : 128 * (i + 1)] = (silu(tile(i)) * tile(3 + i)).astype(BF)
    t = tile(6)
    low = lax.broadcasted_iota(jnp.int32, (128, 128), 1) < 64
    hb[mine, 384:512] = jnp.where(low, silu(t) * pltpu.roll(t, 64, 1), 0.0).astype(BF)

    for e in (1, 3, 2):
        rc(hb.at[mine, :], hb.at[mine, :], hS, hR.at[m], dev(l, (m + e) % 4)).start()
    for i, d in enumerate((0, 1, 3, 2)):
        mi = (y + d) % 4

        @pl.when(mi != m)
        def _():
            rc(pb.at[i], rf.at[m], rfS.at[i], rfR.at[m], dev(l, mi)).wait_send()
            rc(sqs.at[i], sqm.at[m], sqS.at[i], sqR.at[m], dev(l, mi)).wait_send()

    arrived(dwp.at[pl.ds(0, 448), :], dR)

    def y_copy(e, mi):
        to = (l + e) % 4
        at = rows_of(mi, 128)
        return rc(yb.at[at, rows_of(to, COLS)], yr.at[l, at, :], oS, oR.at[l, mi], dev(to, m))

    def last_copy(kp):
        return rc(fs.at[kp], fb.at[k], fS, fR.at[k], (r, kp))

    def finish(mi):
        at = rows_of(mi, 128)
        v = yown[at, :]
        for e in (1, 3, 2):
            lp = (l + e) % 4
            arrived(yr.at[lp, at, :], oR.at[lp, mi])
            v = v + yr[lp, at, :].astype(F32)
        for i in range(2):
            kp = 2 * mi + i
            fs[kp] = v[64 * i : 64 * (i + 1), :].astype(BF)

            @pl.when(kp == k)
            def _():
                ownf[...] = v[64 * i : 64 * (i + 1), :]

            @pl.when(kp != k)
            def _():
                last_copy(kp).start()

    turns = [(m + d) % 4 for d in (0, 1, 3, 2)]
    for i, mi in enumerate(turns):
        at = rows_of(mi, 128)
        if i:
            arrived(hb.at[at, :], hR.at[mi])
        v = dot(hb[at, :], dwp[...])
        yb[at, :] = v.astype(BF)
        for e in (1, 3, 2):
            y_copy(e, mi).start()
        yown[at, :] = dot(hb[at, :], dwp[:, rows_of(l, COLS)])
    for mi in turns:
        finish(mi)

    arrived(hb.at[pl.ds(0, 384), :], hS)
    arrived(yb.at[:, pl.ds(0, 768)], oS)
    res = mid[...] + ownf[...]
    for d in (1, 2, 3, 6, 7, 4, 5):
        kp = peer(d)
        arrived(fb.at[kp], fR.at[kp])
        res = res + fb[kp].astype(F32)
    out[...] = res.astype(BF)
    arrived(fs.at[pl.ds(0, 7)], fS)


def shards(
    residual_in,
    attn_gain,
    query_weight,
    key_matrix,
    value_matrix,
    key_cache,
    cached_values,
    cache_lengths,
    positions,
    output_weight,
    mlp_gain,
    gate_weight,
    up_weight,
    down_weight,
):
    hbm = pl.BlockSpec(memory_space=pltpu.MemorySpace.HBM)
    vmem = pl.BlockSpec(memory_space=pltpu.MemorySpace.VMEM)
    smem = pl.BlockSpec(memory_space=pltpu.MemorySpace.SMEM)
    V = pltpu.VMEM
    dma = lambda *shape: pltpu.SemaphoreType.DMA(shape) if shape else pltpu.SemaphoreType.DMA
    return pl.pallas_call(
        kernel,
        out_shape=jax.ShapeDtypeStruct((64, COLS), BF),
        in_specs=[smem, vmem, hbm, vmem, hbm, hbm, hbm, hbm, hbm, hbm, vmem, hbm, hbm, hbm],
        out_specs=vmem,
        scratch_shapes=[
            V((ROWS, MODEL_WIDTH), BF),
            V((ROWS, MODEL_WIDTH), BF),
            V((MODEL_WIDTH, HEADS * HD), BF),
            V((MODEL_WIDTH, HD), BF),
            V((MODEL_WIDTH, HD), BF),
            V((ROWS, SLOTS, HD), BF),
            V((ROWS, SLOTS, HD), BF),
            V((8 * ROWS, HD), F32),
            V((8 * ROWS, HD), F32),
            V((8 * ROWS, HD), F32),
            V((8 * ROWS, HD), F32),
            V((8 * ROWS, SLOTS), F32),
            V((8 * ROWS, SLOTS), F32),
            V((ROWS, HEADS * HD), BF),
            V((64, MODEL_WIDTH), BF),
            V((MODEL_WIDTH, COLS), BF),
            V((64, COLS), BF),
            V((2, COLS, 128), BF),
            V((2, COLS, 128), BF),
            V((4, COLS, 128), BF),
            V((1024, CHUNK), BF),
            V((512, 1024), BF),
            V((4, 1, COLS), F32),
            V((512, 1024), BF),
            V((64, COLS), F32),
            V((4, 128, CHUNK), BF),
            V((4, 128, CHUNK), BF),
            V((128, CHUNK), F32),
            V((512, 512), BF),
            V((512, 1024), BF),
            V((4, 512, COLS), BF),
            V((512, COLS), F32),
            V((NK, 64, COLS), BF),
            V((NK, 64, COLS), BF),
            V((64, COLS), F32),
            V((4, 8, 128), F32),
            V((4, 8, 128), F32),
            dma(11),
            dma(),
            dma(),
            dma(),
            dma(),
            dma(),
            dma(),
            dma(3),
            dma(4),
            dma(),
            dma(),
            pltpu.SemaphoreType.REGULAR,
            dma(),
            dma(NK),
            dma(),
            dma(4, 4),
            dma(4),
            dma(4),
            dma(4),
            dma(4),
            dma(),
            dma(4),
            dma(),
            dma(4, 4),
            dma(),
            dma(NK),
        ],
        compiler_params=pltpu.CompilerParams(
            collective_id=0, has_side_effects=True, vmem_limit_bytes=56 << 20
        ),
    )(
        cache_lengths,
        positions.reshape(1, ROWS),
        residual_in,
        attn_gain.reshape(1, MODEL_WIDTH),
        query_weight,
        key_matrix,
        value_matrix,
        key_cache.reshape(ROWS, SLOTS, HD),
        cached_values.reshape(ROWS, SLOTS, HD),
        output_weight,
        mlp_gain.reshape(1, COLS),
        gate_weight,
        up_weight,
        down_weight,
    )


def solution(mesh):
    return jax.shard_map(
        shards,
        mesh=mesh,
        in_specs=(
            P(None, "req"),
            P(),
            P(None, "kv"),
            P(None, "kv"),
            P(None, "kv"),
            P("req", "kv", None, None),
            P("req", "kv", None, None),
            P("req"),
            P("req"),
            P(None, "req"),
            P("req"),
            P("req", "kv"),
            P("req", "kv"),
            P("kv", "req"),
        ),
        out_specs=P("kv", "req"),
        check_vma=False,
    )
```

```python
import functools
import math

import jax
import jax.numpy as jnp
from jax import lax
from jax.experimental import pallas as pl
from jax.experimental.pallas import tpu as pltpu
from jax.sharding import PartitionSpec as P

MODEL_WIDTH = 4096
WINDOW = 512
SINKS = 4
EPS = 1e-05
THETA = 10000.0

NR = 16
NK = 8
ROWS = 32
COLS = 256
HEADS = 4
HD = 128
SLOTS = 640
CHUNK = 896

BF = jnp.bfloat16
F32 = jnp.float32
MESH = pl.DeviceIdType.MESH
NT = (((1,), (1,)), ((), ()))
TN = (((0,), (0,)), ((), ()))


def dot(a, b):
    return jnp.dot(a, b, preferred_element_type=F32)


def piece_offset(l):
    return 448 * l + 64 * (l % 2)


def kernel(
    lens, pos, resid, gain1, wq, wk, wv, kc, vc, wo, gain2, gw, uw, dw,
    out,
    tok, nrm, wq_v, wk_v, wv_v, k_v, v_v, q3, k3, v3, o3, s3, w3, att, attb, wo_v, res_v,
    gp, up, pk, wp, dwp, gl, al, mid, pb, rf, hb, yb, yr, fs, fb, invs, sqm,
    ld, tokS, tokR, wS, wR, dS, dR, gS, gR, attS, attR, b2, yS, yR, lS, alR, sqS, sqR,
    rfS, rfR, hS, hR, oS, oR, fS, fR,
):
    r = lax.axis_index("req")
    k = lax.axis_index("kv")
    x, z = r // 4, r % 4
    y, c = k // 2, k % 2
    l = (1 - c) * x + c * z
    m = (1 - c) * z + c * x

    def dev(li, mi):
        return ((1 - c) * (4 * li + mi) + c * (4 * mi + li), k)

    def rc(src, dst, ss, rs, to):
        return pltpu.make_async_remote_copy(
            src_ref=src, dst_ref=dst, send_sem=ss, recv_sem=rs, device_id=to, device_id_type=MESH
        )

    def arrived(ref, sem):
        pltpu.make_async_copy(ref, ref, sem).wait()

    def rows_of(i, n):
        return pl.ds(pl.multiple_of(n * i, n), n)

    barrier = pltpu.get_barrier_semaphore()
    for d in range(1, NR):
        pl.semaphore_signal(barrier, inc=1, device_id=((r + d) % NR, k), device_id_type=MESH)
    for d in range(1, NK):
        pl.semaphore_signal(barrier, inc=1, device_id=(r, (k + d) % NK), device_id_type=MESH)

    loads = {}

    def load(name, src, dst):
        loads[name] = pltpu.make_async_copy(src, dst, ld.at[len(loads)])
        loads[name].start()

    pltpu.make_async_copy(resid.at[rows_of(r, ROWS), :], tok.at[:, rows_of(r, COLS)], tokR).start()
    load("g3", gw.at[:, pl.ds(384, 128)], gp.at[0])
    load("g10", gw.at[:, pl.ds(1280, 128)], gp.at[1])
    load("u3", uw.at[:, pl.ds(384, 128)], up.at[0])
    load("u10", uw.at[:, pl.ds(1280, 128)], up.at[1])
    load("wq", wq, wq_v)
    load("wk", wk, wk_v)
    load("wv", wv, wv_v)
    load("kc", kc, k_v)
    load("vc", vc, v_v)
    load("wo", wo, wo_v)
    load("res", resid.at[rows_of(k, 64), :], res_v)

    pl.semaphore_wait(barrier, NR - 1 + NK - 1)

    for d in range(1, NR):
        to = (r + d) % NR
        rc(resid.at[rows_of(to, ROWS), :], tok.at[:, rows_of(r, COLS)], tokS, tokR, (to, k)).start()
    for d in range(1, NK):
        pl.semaphore_signal(b2, inc=1, device_id=(r, (k + d) % NK), device_id_type=MESH)

    def w_copies(d):
        to = (l + d) % 4
        off = pl.multiple_of(piece_offset(to), 128)
        here = rows_of(l, COLS)
        pieces = (
            (gw.at[:, pl.ds(off, 384)], wp.at[here, pl.ds(0, 384)]),
            (uw.at[:, pl.ds(off, 384)], wp.at[here, pl.ds(384, 384)]),
            (pk.at[to], wp.at[here, pl.ds(768, 128)]),
        )
        if d == 0:
            return [pltpu.make_async_copy(s, t, wR) for s, t in pieces]
        return [rc(s, t, wS, wR, dev(to, m)) for s, t in pieces]

    def d_copies(d):
        to = (l + d) % 4
        off = pl.multiple_of(piece_offset(to), 64)
        off2 = pl.multiple_of(384 + 896 * (to // 2) + 64 * (to % 2), 64)
        here = rows_of(l, COLS)
        pieces = (
            (dw.at[pl.ds(off, 384), :], dwp.at[pl.ds(0, 384), here]),
            (dw.at[pl.ds(off2, 64), :], dwp.at[pl.ds(384, 64), here]),
        )
        if d == 0:
            return [pltpu.make_async_copy(s, t, dR) for s, t in pieces]
        return [rc(s, t, dS, dR, dev(to, m)) for s, t in pieces]

    w_sends = {d: w_copies(d) for d in range(4)}
    for d in (1, 3, 2, 0):
        w_sends[d][0].start()
        w_sends[d][1].start()
    for name in ("g3", "g10", "u3", "u10"):
        loads[name].wait()
    low = lax.broadcasted_iota(jnp.int32, (COLS, 128), 1) < 64
    for t in range(2):
        g = gp[t].astype(F32)
        u = up[t].astype(F32)
        pk[2 * t] = jnp.where(low, g, pltpu.roll(u, 64, 1)).astype(BF)
        pk[2 * t + 1] = jnp.where(low, pltpu.roll(g, 64, 1), u).astype(BF)
    for d in (1, 3, 2, 0):
        w_sends[d][2].start()
    gl[l] = gain2[...]
    for d in range(1, 4):
        rc(gain2, gl.at[l], gS.at[d - 1], gR.at[l], dev((l + d) % 4, m)).start()

    q3[...] = jnp.zeros_like(q3)
    k3[...] = jnp.zeros_like(k3)
    v3[...] = jnp.zeros_like(v3)
    dwp[448:512, :] = jnp.zeros((64, 1024), BF)

    sub = lax.broadcasted_iota(jnp.int32, (8, 128), 0)
    lane = lax.broadcasted_iota(jnp.int32, (ROWS, HD), 1)
    p8 = jnp.broadcast_to(pos[...].astype(F32), (8, ROWS))
    place = lax.dot_general(
        p8, (sub == 0).astype(F32), TN, preferred_element_type=F32, precision=lax.Precision.HIGHEST
    )
    freq = jnp.exp((lane % 64).astype(F32) * (-2.0 * math.log(THETA) / HD))
    angle = place * freq
    cs = jnp.cos(angle)
    sn = jnp.where(lane < 64, -1.0, 1.0) * jnp.sin(angle)

    arrived(tok, tokR)
    t = tok[...].astype(F32)
    scale = 1.0 / jnp.sqrt(jnp.sum(t * t, axis=-1, keepdims=True) / MODEL_WIDTH + EPS)
    nrm[...] = (t * scale * gain1[...]).astype(BF)
    loads["wq"].wait()
    loads["wk"].wait()
    loads["wv"].wait()
    q = dot(nrm[...], wq_v[...])
    kn = dot(nrm[...], wk_v[...])
    vn = dot(nrm[...], wv_v[...])

    def rotate(v):
        return (v * cs + pltpu.roll(v, 64, 1) * sn).astype(BF).astype(F32)

    kn = rotate(kn)
    vn = vn.astype(BF).astype(F32)
    for h in range(HEADS):
        q3[pl.ds(h, ROWS, stride=8), :] = rotate(q[:, HD * h : HD * (h + 1)])
        k3[pl.ds(h, ROWS, stride=8), :] = kn
        v3[pl.ds(h, ROWS, stride=8), :] = vn

    factor = 1.0 / math.sqrt(HD)
    slot = lax.broadcasted_iota(jnp.int32, (8, SLOTS), 1)
    loads["kc"].wait()
    for half in range(2):
        for b in range(16 * half, 16 * half + 16):
            rows = slice(8 * b, 8 * b + 8)
            s = lax.dot_general(q3[rows, :].astype(BF), k_v[b], NT, preferred_element_type=F32)
            n = lens[b]
            ok = (slot < n) & ((slot < SINKS) | (slot > n - WINDOW))
            s3[rows, :] = jnp.where(ok, s * factor, -1e30)
        rows = slice(128 * half, 128 * half + 128)
        s = s3[rows, :]
        own = jnp.sum(q3[rows, :] * k3[rows, :], axis=-1, keepdims=True) * factor
        peak = jnp.maximum(jnp.max(s, axis=-1, keepdims=True), own)
        e = jnp.where(s > -1e29, jnp.exp(s - peak), 0.0)
        eo = jnp.exp(own - peak)
        inv = 1.0 / (jnp.sum(e, axis=-1, keepdims=True) + eo)
        w3[rows, :] = e * inv
        o3[rows, :] = (eo * inv).astype(BF).astype(F32) * v3[rows, :]
        if half == 0:
            loads["vc"].wait()
        for b in range(16 * half, 16 * half + 16):
            rows = slice(8 * b, 8 * b + 8)
            o3[rows, :] += dot(w3[rows, :].astype(BF), v_v[b])
    for h in range(HEADS):
        att[:, HD * h : HD * (h + 1)] = o3[pl.ds(h, ROWS, stride=8), :].astype(BF)

    kd = r // 2
    there = attb.at[rows_of(r % 2, ROWS), rows_of(k, 512)]
    pl.semaphore_wait(b2, NK - 1)

    @pl.when(k == kd)
    def _():
        pltpu.make_async_copy(att, there, attR).start()

    @pl.when(k != kd)
    def _():
        rc(att, there, attS, attR, (r, kd)).start()

    for d in range(1, NR):
        rc(att, there, attS, attR, ((r + d) % NR, kd)).start()

    arrived(tok.at[:, pl.ds(0, COLS * 15)], tokS)
    arrived(wp.at[pl.ds(0, 768), :], wS)
    for d in range(1, 4):
        rc(gain2, gl.at[l], gS.at[d - 1], gR.at[l], dev((l + d) % 4, m)).wait_send()

    loads["wo"].wait()
    loads["res"].wait()
    arrived(attb, attR)
    for d in (1, 3, 2, 0):
        for copy in d_copies(d):
            copy.start()
    o = res_v[...].astype(F32) + dot(attb[...], wo_v[...])
    mid[...] = o
    mine = rows_of(y, 64)
    mycols = rows_of(l, COLS)
    al[c, mine, mycols] = (o * gain2[...]).astype(BF)

    around = (1, 3, 2)

    def kv_send(kp):
        cp = kp % 2
        lp = (1 - cp) * x + cp * z
        rc(al.at[c, mine, mycols], al.at[c, mine, rows_of(lp, COLS)], yS, yR.at[k], (r, kp)).start()

    def line_sends(h, yp):
        block = al.at[h, rows_of(yp, 64), mycols]
        for e in around:
            rc(block, block, lS, alR.at[h, l], dev((l + e) % 4, m)).start()

    halves = (c, 1 - c)
    for e in around:
        kv_send(2 * ((y + e) % 4) + c)
    for e in (0,) + around:
        kv_send(2 * ((y + e) % 4) + 1 - c)
    line_sends(c, y)
    for i, h in enumerate(halves):
        for e in around if i == 0 else (0,) + around:
            yp = (y + e) % 4
            kp = 2 * yp + h
            arrived(al.at[h, rows_of(yp, 64), mycols], yR.at[kp])
            line_sends(h, yp)

    @pl.when(k == kd)
    def _():
        arrived(attb.at[pl.ds(0, 32), pl.ds(0, 3584)], attS)
        arrived(attb.at[pl.ds(32, 32), pl.ds(0, 4096)], attS)

    @pl.when(k != kd)
    def _():
        arrived(attb, attS)

    arrived(wp, wR)
    for d in range(1, 4):
        at = (l + d) % 4
        arrived(gl.at[at], gR.at[at])
    ginv = [1.0 / gl[i] for i in range(4)]
    my64 = rows_of(m, 64)

    def gate(h):
        for e in around:
            lp = (l + e) % 4
            arrived(al.at[h, :, rows_of(lp, COLS)], alR.at[h, lp])
        pb[h] = dot(al[h], wp[...]).astype(BF)
        for e in around:
            mi = (m + e) % 4
            rc(pb.at[h, rows_of(mi, 64), :], rf.at[h, m], rfS, rfR.at[h, m], dev(l, mi)).start()
        part = jnp.zeros((256, 128), F32)
        for j in range(8):
            g = ginv[j // 2][:, 128 * (j % 2) : 128 * (j % 2) + 128]
            v = al[h, :, 128 * j : 128 * (j + 1)].astype(F32) * g
            part = part + v * v
        sqm[h, m] = lax.dot_general(
            jnp.ones((8, 128), F32), part, NT, preferred_element_type=F32, precision=lax.Precision.HIGHEST
        )
        for e in around:
            mi = (m + e) % 4
            rc(sqm.at[h, m], sqm.at[h, m], sqS, sqR.at[h, m], dev(l, mi)).start()

    def silu(v):
        return v / (1.0 + jnp.exp(-v))

    def hide(h):
        for e in around:
            mi = (m + e) % 4
            arrived(sqm.at[h, mi], sqR.at[h, mi])
        total = lax.dot_general(
            sqm[h, 0] + sqm[h, 1] + sqm[h, 2] + sqm[h, 3],
            (sub == 0).astype(F32),
            TN,
            preferred_element_type=F32,
            precision=lax.Precision.HIGHEST,
        )
        invs[...] = 1.0 / jnp.sqrt(total / MODEL_WIDTH + EPS)
        inv = invs[my64, :]
        for e in around:
            mi = (m + e) % 4
            arrived(rf.at[h, mi], rfR.at[h, mi])

        def tile(i):
            at = slice(128 * i, 128 * (i + 1))
            v = pb[h, my64, at].astype(F32)
            for e in around:
                v = v + rf[h, (m + e) % 4, :, at].astype(F32)
            return v * inv

        for i in range(3):
            hb[h, my64, 128 * i : 128 * (i + 1)] = (silu(tile(i)) * tile(3 + i)).astype(BF)
        t = tile(6)
        low = lax.broadcasted_iota(jnp.int32, (64, 128), 1) < 64
        hb[h, my64, 384:512] = jnp.where(low, silu(t) * pltpu.roll(t, 64, 1), 0.0).astype(BF)
        for e in around:
            rc(hb.at[h, my64, :], hb.at[h, my64, :], hS, hR.at[h, m], dev(l, (m + e) % 4)).start()

    for h in halves:
        gate(h)
    for h in halves:
        hide(h)

    arrived(hb.at[0, pl.ds(0, 224), :], yS)
    arrived(al.at[:, :, pl.ds(0, 768)], lS)
    arrived(pb.at[:, pl.ds(0, 192), :], rfS)
    arrived(sqm.at[:, pl.ds(0, 3)], sqS)
    arrived(dwp.at[pl.ds(0, 448), pl.ds(0, 768)], dS)
    arrived(dwp.at[pl.ds(0, 448), :], dR)

    def down(h):
        for e in around:
            mi = (m + e) % 4
            arrived(hb.at[h, rows_of(mi, 64), :], hR.at[h, mi])
        yb[h] = dot(hb[h], dwp[...]).astype(BF)
        for e in around:
            to = (l + e) % 4
            rc(yb.at[h, :, rows_of(to, COLS)], yr.at[h, l], oS, oR.at[h, l], dev(to, m)).start()

    def finish(i, h):
        v = yb[h, :, mycols].astype(F32)
        for e in around:
            lp = (l + e) % 4
            arrived(yr.at[h, lp], oR.at[h, lp])
            v = v + yr[h, lp].astype(F32)
        fs[h] = v.astype(BF)
        for e in around if i == 0 else (0,) + around:
            yp = (y + e) % 4
            rc(fs.at[h, rows_of(yp, 64), :], fb.at[k], fS, fR.at[k], (r, 2 * yp + h)).start()

    for h in halves:
        down(h)
    for i, h in enumerate(halves):
        finish(i, h)
    arrived(hb.at[:, pl.ds(0, 192), :], hS)
    arrived(yb.at[:, :, pl.ds(0, 768)], oS)
    res = mid[...] + fs[c, mine, :].astype(F32)
    for i, h in enumerate(halves):
        for e in around if i == 0 else (0,) + around:
            kp = 2 * ((y + e) % 4) + h
            arrived(fb.at[kp], fR.at[kp])
            res = res + fb[kp].astype(F32)
    out[...] = res.astype(BF)
    arrived(yb.at[0, pl.ds(0, 112), :], fS)


def shards(
    residual_in,
    attn_gain,
    query_weight,
    key_matrix,
    value_matrix,
    key_cache,
    cached_values,
    cache_lengths,
    positions,
    output_weight,
    mlp_gain,
    gate_weight,
    up_weight,
    down_weight,
):
    hbm = pl.BlockSpec(memory_space=pltpu.MemorySpace.HBM)
    vmem = pl.BlockSpec(memory_space=pltpu.MemorySpace.VMEM)
    smem = pl.BlockSpec(memory_space=pltpu.MemorySpace.SMEM)
    V = pltpu.VMEM
    dma = lambda *shape: pltpu.SemaphoreType.DMA(shape) if shape else pltpu.SemaphoreType.DMA
    return pl.pallas_call(
        kernel,
        out_shape=jax.ShapeDtypeStruct((64, COLS), BF),
        in_specs=[smem, vmem, hbm, vmem, hbm, hbm, hbm, hbm, hbm, hbm, vmem, hbm, hbm, hbm],
        out_specs=vmem,
        scratch_shapes=[
            V((ROWS, MODEL_WIDTH), BF),
            V((ROWS, MODEL_WIDTH), BF),
            V((MODEL_WIDTH, HEADS * HD), BF),
            V((MODEL_WIDTH, HD), BF),
            V((MODEL_WIDTH, HD), BF),
            V((ROWS, SLOTS, HD), BF),
            V((ROWS, SLOTS, HD), BF),
            V((8 * ROWS, HD), F32),
            V((8 * ROWS, HD), F32),
            V((8 * ROWS, HD), F32),
            V((8 * ROWS, HD), F32),
            V((8 * ROWS, SLOTS), F32),
            V((8 * ROWS, SLOTS), F32),
            V((ROWS, HEADS * HD), BF),
            V((64, MODEL_WIDTH), BF),
            V((MODEL_WIDTH, COLS), BF),
            V((64, COLS), BF),
            V((2, COLS, 128), BF),
            V((2, COLS, 128), BF),
            V((4, COLS, 128), BF),
            V((1024, CHUNK), BF),
            V((512, 1024), BF),
            V((4, 1, COLS), F32),
            V((2, 256, 1024), BF),
            V((64, COLS), F32),
            V((2, 256, CHUNK), BF),
            V((2, 4, 64, CHUNK), BF),
            V((2, 256, 512), BF),
            V((2, 256, 1024), BF),
            V((2, 4, 256, COLS), BF),
            V((2, 256, COLS), BF),
            V((NK, 64, COLS), BF),
            V((256, 128), F32),
            V((2, 4, 8, 256), F32),
            dma(11),
            dma(),
            dma(),
            dma(),
            dma(),
            dma(),
            dma(),
            dma(3),
            dma(4),
            dma(),
            dma(),
            pltpu.SemaphoreType.REGULAR,
            dma(),
            dma(NK),
            dma(),
            dma(2, 4),
            dma(),
            dma(2, 4),
            dma(),
            dma(2, 4),
            dma(),
            dma(2, 4),
            dma(),
            dma(2, 4),
            dma(),
            dma(NK),
        ],
        compiler_params=pltpu.CompilerParams(
            collective_id=0, has_side_effects=True, vmem_limit_bytes=56 << 20
        ),
    )(
        cache_lengths,
        positions.reshape(1, ROWS),
        residual_in,
        attn_gain.reshape(1, MODEL_WIDTH),
        query_weight,
        key_matrix,
        value_matrix,
        key_cache.reshape(ROWS, SLOTS, HD),
        cached_values.reshape(ROWS, SLOTS, HD),
        output_weight,
        mlp_gain.reshape(1, COLS),
        gate_weight,
        up_weight,
        down_weight,
    )


def solution(mesh):
    return jax.shard_map(
        shards,
        mesh=mesh,
        in_specs=(
            P(None, "req"),
            P(),
            P(None, "kv"),
            P(None, "kv"),
            P(None, "kv"),
            P("req", "kv", None, None),
            P("req", "kv", None, None),
            P("req"),
            P("req"),
            P(None, "req"),
            P("req"),
            P("req", "kv"),
            P("req", "kv"),
            P("kv", "req"),
        ),
        out_specs=P("kv", "req"),
        check_vma=False,
    )
```

```python
import functools
import math

import jax
import jax.numpy as jnp
from jax import lax
from jax.experimental import pallas as pl
from jax.experimental.pallas import tpu as pltpu
from jax.sharding import PartitionSpec as P

MODEL_WIDTH = 4096
WINDOW = 512
SINKS = 4
EPS = 1e-05
THETA = 10000.0

NR = 16
NK = 8
ROWS = 32
COLS = 256
HEADS = 4
HD = 128
SLOTS = 640
CHUNK = 896

BF = jnp.bfloat16
F32 = jnp.float32
MESH = pl.DeviceIdType.MESH
NT = (((1,), (1,)), ((), ()))
TN = (((0,), (0,)), ((), ()))


def dot(a, b):
    return jnp.dot(a, b, preferred_element_type=F32)


def piece_offset(l):
    return 448 * l + 64 * (l % 2)


def kernel(
    lens, pos, resid, gain1, wq, wk, wv, kc, vc, wo, gain2, gw, uw, dw,
    out,
    tok, nrm, wq_v, wk_v, wv_v, k_v, v_v, q3, k3, v3, o3, s3, w3, att, attb, wo_v, res_v,
    gp, up, pk, wp, dwp, gl, al, mid, pb, rf, hb, yb, yr, vf, fs, fb, invs, sqm, mb,
    ld, tokS, tokR, wS, wR, dS, dR, gS, gR, attS, attR, b2, yS, yR, lS, alR, sqS, sqR,
    rfS, rfR, hS, hR, oS, oR, fS, fR, swS, swR, sdS, sdR,
):
    r = lax.axis_index("req")
    k = lax.axis_index("kv")
    x, z = r // 4, r % 4
    y, c = k // 2, k % 2
    l = (1 - c) * x + c * z
    m = (1 - c) * z + c * x

    def dev(li, mi):
        return ((1 - c) * (4 * li + mi) + c * (4 * mi + li), k)

    def places(j):
        return (1 - j) * x + j * z, (1 - j) * z + j * x

    def devj(j, li, mi):
        return ((1 - j) * (4 * li + mi) + j * (4 * mi + li), k)

    sibling = (r, 2 * y + 1 - c)

    def rc(src, dst, ss, rs, to):
        return pltpu.make_async_remote_copy(
            src_ref=src, dst_ref=dst, send_sem=ss, recv_sem=rs, device_id=to, device_id_type=MESH
        )

    def arrived(ref, sem):
        pltpu.make_async_copy(ref, ref, sem).wait()

    def rows_of(i, n):
        return pl.ds(pl.multiple_of(n * i, n), n)

    barrier = pltpu.get_barrier_semaphore()
    for d in range(1, NR):
        pl.semaphore_signal(barrier, inc=1, device_id=((r + d) % NR, k), device_id_type=MESH)
    for d in range(1, NK):
        pl.semaphore_signal(barrier, inc=1, device_id=(r, (k + d) % NK), device_id_type=MESH)

    loads = {}

    def load(name, src, dst):
        loads[name] = pltpu.make_async_copy(src, dst, ld.at[len(loads)])
        loads[name].start()

    pltpu.make_async_copy(resid.at[rows_of(r, ROWS), :], tok.at[:, rows_of(r, COLS)], tokR).start()
    load("g3", gw.at[:, pl.ds(384, 128)], gp.at[0])
    load("g10", gw.at[:, pl.ds(1280, 128)], gp.at[1])
    load("u3", uw.at[:, pl.ds(384, 128)], up.at[0])
    load("u10", uw.at[:, pl.ds(1280, 128)], up.at[1])
    load("wq", wq, wq_v)
    load("wk", wk, wk_v)
    load("wv", wv, wv_v)
    load("kc", kc, k_v)
    load("vc", vc, v_v)
    load("wo", wo, wo_v)
    load("res", resid.at[rows_of(k, 64), :], res_v)

    pl.semaphore_wait(barrier, NR - 1 + NK - 1)

    for d in range(1, NR):
        to = (r + d) % NR
        rc(resid.at[rows_of(to, ROWS), :], tok.at[:, rows_of(r, COLS)], tokS, tokR, (to, k)).start()
    for d in range(1, NK):
        pl.semaphore_signal(b2, inc=1, device_id=(r, (k + d) % NK), device_id_type=MESH)

    def w_copies(d):
        to = (l + d) % 4
        off = pl.multiple_of(piece_offset(to), 128)
        here = rows_of(l, COLS)
        pieces = (
            (gw.at[:, pl.ds(off, 384)], wp.at[c, here, pl.ds(0, 384)]),
            (uw.at[:, pl.ds(off, 384)], wp.at[c, here, pl.ds(384, 384)]),
            (pk.at[to], wp.at[c, here, pl.ds(768, 128)]),
        )
        if d == 0:
            return [pltpu.make_async_copy(s, t, wR) for s, t in pieces]
        return [rc(s, t, wS, wR, dev(to, m)) for s, t in pieces]

    def d_copies(d):
        to = (l + d) % 4
        off = pl.multiple_of(piece_offset(to), 64)
        off2 = pl.multiple_of(384 + 896 * (to // 2) + 64 * (to % 2), 64)
        here = rows_of(l, COLS)
        pieces = (
            (dw.at[pl.ds(off, 384), :], dwp.at[c, pl.ds(0, 384), here]),
            (dw.at[pl.ds(off2, 64), :], dwp.at[c, pl.ds(384, 64), here]),
        )
        if d == 0:
            return [pltpu.make_async_copy(s, t, dR) for s, t in pieces]
        return [rc(s, t, dS, dR, dev(to, m)) for s, t in pieces]

    w_sends = {d: w_copies(d) for d in range(4)}
    for d in (1, 3, 2, 0):
        w_sends[d][0].start()
        w_sends[d][1].start()
    for name in ("g3", "g10", "u3", "u10"):
        loads[name].wait()
    low = lax.broadcasted_iota(jnp.int32, (COLS, 128), 1) < 64
    for t in range(2):
        g = gp[t].astype(F32)
        u = up[t].astype(F32)
        pk[2 * t] = jnp.where(low, g, pltpu.roll(u, 64, 1)).astype(BF)
        pk[2 * t + 1] = jnp.where(low, pltpu.roll(g, 64, 1), u).astype(BF)
    for d in (1, 3, 2, 0):
        w_sends[d][2].start()
    def gain_copies():
        out = []
        for j in range(2):
            lj, mj = places(j)
            for d in range(1, 4):
                to = devj(j, (lj + d) % 4, mj)
                out.append(rc(gain2, gl.at[j, lj], gS.at[j, d - 1], gR.at[j, lj], to))
        return out

    for j in range(2):
        gl[j, places(j)[0]] = gain2[...]
    for copy in gain_copies():
        copy.start()

    q3[...] = jnp.zeros_like(q3)
    k3[...] = jnp.zeros_like(k3)
    v3[...] = jnp.zeros_like(v3)
    for j in range(2):
        dwp[j, 448:512, :] = jnp.zeros((64, 1024), BF)

    sub = lax.broadcasted_iota(jnp.int32, (8, 128), 0)
    lane = lax.broadcasted_iota(jnp.int32, (ROWS, HD), 1)
    p8 = jnp.broadcast_to(pos[...].astype(F32), (8, ROWS))
    place = lax.dot_general(
        p8, (sub == 0).astype(F32), TN, preferred_element_type=F32, precision=lax.Precision.HIGHEST
    )
    freq = jnp.exp((lane % 64).astype(F32) * (-2.0 * math.log(THETA) / HD))
    angle = place * freq
    cs = jnp.cos(angle)
    sn = jnp.where(lane < 64, -1.0, 1.0) * jnp.sin(angle)

    arrived(tok, tokR)
    t = tok[...].astype(F32)
    scale = 1.0 / jnp.sqrt(jnp.sum(t * t, axis=-1, keepdims=True) / MODEL_WIDTH + EPS)
    nrm[...] = (t * scale * gain1[...]).astype(BF)
    loads["wq"].wait()
    loads["wk"].wait()
    loads["wv"].wait()
    q = dot(nrm[...], wq_v[...])
    kn = dot(nrm[...], wk_v[...])
    vn = dot(nrm[...], wv_v[...])

    def rotate(v):
        return (v * cs + pltpu.roll(v, 64, 1) * sn).astype(BF).astype(F32)

    kn = rotate(kn)
    vn = vn.astype(BF).astype(F32)
    for h in range(HEADS):
        q3[pl.ds(h, ROWS, stride=8), :] = rotate(q[:, HD * h : HD * (h + 1)])
        k3[pl.ds(h, ROWS, stride=8), :] = kn
        v3[pl.ds(h, ROWS, stride=8), :] = vn

    factor = 1.0 / math.sqrt(HD)
    slot = lax.broadcasted_iota(jnp.int32, (8, SLOTS), 1)
    loads["kc"].wait()
    for half in range(2):
        for b in range(16 * half, 16 * half + 16):
            rows = slice(8 * b, 8 * b + 8)
            s = lax.dot_general(q3[rows, :].astype(BF), k_v[b], NT, preferred_element_type=F32)
            n = lens[b]
            ok = (slot < n) & ((slot < SINKS) | (slot > n - WINDOW))
            s3[rows, :] = jnp.where(ok, s * factor, -1e30)
        rows = slice(128 * half, 128 * half + 128)
        s = s3[rows, :]
        own = jnp.sum(q3[rows, :] * k3[rows, :], axis=-1, keepdims=True) * factor
        peak = jnp.maximum(jnp.max(s, axis=-1, keepdims=True), own)
        e = jnp.where(s > -1e29, jnp.exp(s - peak), 0.0)
        eo = jnp.exp(own - peak)
        inv = 1.0 / (jnp.sum(e, axis=-1, keepdims=True) + eo)
        w3[rows, :] = e * inv
        o3[rows, :] = (eo * inv).astype(BF).astype(F32) * v3[rows, :]
        if half == 0:
            loads["vc"].wait()
        for b in range(16 * half, 16 * half + 16):
            rows = slice(8 * b, 8 * b + 8)
            o3[rows, :] += dot(w3[rows, :].astype(BF), v_v[b])
    for h in range(HEADS):
        att[:, HD * h : HD * (h + 1)] = o3[pl.ds(h, ROWS, stride=8), :].astype(BF)

    kd = r // 2
    there = attb.at[rows_of(r % 2, ROWS), rows_of(k, 512)]
    pl.semaphore_wait(b2, NK - 1)

    @pl.when(k == kd)
    def _():
        pltpu.make_async_copy(att, there, attR).start()

    @pl.when(k != kd)
    def _():
        rc(att, there, attS, attR, (r, kd)).start()

    for d in range(1, NR):
        rc(att, there, attS, attR, ((r + d) % NR, kd)).start()

    arrived(tok.at[:, pl.ds(0, COLS * 15)], tokS)
    arrived(wp.at[c, pl.ds(0, 768), :], wS)
    for copy in gain_copies():
        copy.wait_send()

    loads["wo"].wait()
    loads["res"].wait()
    arrived(attb, attR)
    for d in (1, 3, 2, 0):
        for copy in d_copies(d):
            copy.start()
    arrived(wp.at[c], wR)
    rc(wp.at[c], wp.at[c], swS, swR, sibling).start()
    o = res_v[...].astype(F32) + dot(attb[...], wo_v[...])
    mid[...] = o
    mine = rows_of(y, 64)
    mb[mine, :] = (o * gain2[...]).astype(BF)

    around = (1, 3, 2)
    sets = (c, 1 - c)

    def line_sends(j, yp):
        lj, mj = places(j)
        at = rows_of(yp, 64)
        for e in around:
            rc(mb.at[at, :], al.at[j, at, rows_of(lj, COLS)], lS, alR.at[j, lj], devj(j, (lj + e) % 4, mj)).start()

    for e in around:
        rc(mb.at[mine, :], mb.at[mine, :], yS, yR.at[y], (r, 2 * ((y + e) % 4) + c)).start()
    for j in sets:
        line_sends(j, y)
    for i, j in enumerate(sets):
        for e in around:
            yp = (y + e) % 4
            if i == 0:
                arrived(mb.at[rows_of(yp, 64), :], yR.at[yp])
            line_sends(j, yp)
    for j in range(2):
        al[j, :, rows_of(places(j)[0], COLS)] = mb[...]

    @pl.when(k == kd)
    def _():
        arrived(attb.at[pl.ds(0, 32), pl.ds(0, 3584)], attS)
        arrived(attb.at[pl.ds(32, 32), pl.ds(0, 4096)], attS)

    @pl.when(k != kd)
    def _():
        arrived(attb, attS)

    def silu(v):
        return v / (1.0 + jnp.exp(-v))

    def gate(j):
        lj, mj = places(j)
        for e in around:
            lp = (lj + e) % 4
            arrived(al.at[j, :, rows_of(lp, COLS)], alR.at[j, lp])
        pb[j] = dot(al[j], wp[j]).astype(BF)
        for e in around:
            mi = (mj + e) % 4
            rc(pb.at[j, rows_of(mi, 64), :], rf.at[j, mj], rfS, rfR.at[j, mj], devj(j, lj, mi)).start()
        for e in around:
            at = (lj + e) % 4
            arrived(gl.at[j, at], gR.at[j, at])
        part = jnp.zeros((256, 128), F32)
        for i in range(8):
            g = 1.0 / gl[j, i // 2, :, 128 * (i % 2) : 128 * (i % 2) + 128]
            v = al[j, :, 128 * i : 128 * (i + 1)].astype(F32) * g
            part = part + v * v
        sqm[j, mj] = lax.dot_general(
            jnp.ones((8, 128), F32), part, NT, preferred_element_type=F32, precision=lax.Precision.HIGHEST
        )
        for e in around:
            mi = (mj + e) % 4
            rc(sqm.at[j, mj], sqm.at[j, mj], sqS, sqR.at[j, mj], devj(j, lj, mi)).start()

    def hide(j):
        lj, mj = places(j)
        here = rows_of(mj, 64)
        for e in around:
            mi = (mj + e) % 4
            arrived(sqm.at[j, mi], sqR.at[j, mi])
        total = lax.dot_general(
            sqm[j, 0] + sqm[j, 1] + sqm[j, 2] + sqm[j, 3],
            (sub == 0).astype(F32),
            TN,
            preferred_element_type=F32,
            precision=lax.Precision.HIGHEST,
        )
        invs[...] = 1.0 / jnp.sqrt(total / MODEL_WIDTH + EPS)
        inv = invs[here, :]
        for e in around:
            mi = (mj + e) % 4
            arrived(rf.at[j, mi], rfR.at[j, mi])

        def tile(i):
            at = slice(128 * i, 128 * (i + 1))
            v = pb[j, here, at].astype(F32)
            for e in around:
                v = v + rf[j, (mj + e) % 4, :, at].astype(F32)
            return v * inv

        for i in range(3):
            hb[j, here, 128 * i : 128 * (i + 1)] = (silu(tile(i)) * tile(3 + i)).astype(BF)
        t = tile(6)
        low = lax.broadcasted_iota(jnp.int32, (64, 128), 1) < 64
        hb[j, here, 384:512] = jnp.where(low, silu(t) * pltpu.roll(t, 64, 1), 0.0).astype(BF)
        for e in around:
            rc(hb.at[j, here, :], hb.at[j, here, :], hS, hR.at[j, mj], devj(j, lj, (mj + e) % 4)).start()

    gate(c)
    arrived(wp.at[1 - c], swR)
    gate(1 - c)
    arrived(dwp.at[c, pl.ds(0, 448), :], dR)
    rc(dwp.at[c, pl.ds(0, 448), :], dwp.at[c, pl.ds(0, 448), :], sdS, sdR, sibling).start()
    for j in sets:
        hide(j)

    arrived(wp.at[c], swS)
    arrived(mb.at[pl.ds(0, 192), :], yS)
    arrived(al.at[:, :, pl.ds(0, 768)], lS)
    arrived(pb.at[:, pl.ds(0, 192), :], rfS)
    arrived(sqm.at[:, pl.ds(0, 3)], sqS)
    arrived(dwp.at[c, pl.ds(0, 448), pl.ds(0, 768)], dS)

    def down(j):
        lj, mj = places(j)
        for e in around:
            mi = (mj + e) % 4
            arrived(hb.at[j, rows_of(mi, 64), :], hR.at[j, mi])
        yb[j] = dot(hb[j], dwp[j]).astype(BF)
        for e in around:
            to = (lj + e) % 4
            rc(yb.at[j, :, rows_of(to, COLS)], yr.at[j, lj], oS, oR.at[j, lj], devj(j, to, mj)).start()

    down(c)
    arrived(dwp.at[1 - c, pl.ds(0, 448), :], sdR)
    down(1 - c)
    v = jnp.zeros((256, COLS), F32)
    for j in sets:
        lj, mj = places(j)
        v = v + yb[j, :, rows_of(lj, COLS)].astype(F32)
        for e in around:
            lp = (lj + e) % 4
            arrived(yr.at[j, lp], oR.at[j, lp])
            v = v + yr[j, lp].astype(F32)
    vf[...] = v
    fs[...] = v.astype(BF)
    for e in around:
        yp = (y + e) % 4
        rc(fs.at[rows_of(yp, 64), :], fb.at[y], fS, fR.at[y], (r, 2 * yp + c)).start()
    arrived(hb.at[:, pl.ds(0, 192), :], hS)
    arrived(yb.at[:, :, pl.ds(0, 768)], oS)
    arrived(dwp.at[c, pl.ds(0, 448), :], sdS)
    res = mid[...] + vf[mine, :]
    for e in around:
        yp = (y + e) % 4
        arrived(fb.at[yp], fR.at[yp])
        res = res + fb[yp].astype(F32)
    out[...] = res.astype(BF)
    arrived(fs.at[pl.ds(0, 192), :], fS)


def shards(
    residual_in,
    attn_gain,
    query_weight,
    key_matrix,
    value_matrix,
    key_cache,
    cached_values,
    cache_lengths,
    positions,
    output_weight,
    mlp_gain,
    gate_weight,
    up_weight,
    down_weight,
):
    hbm = pl.BlockSpec(memory_space=pltpu.MemorySpace.HBM)
    vmem = pl.BlockSpec(memory_space=pltpu.MemorySpace.VMEM)
    smem = pl.BlockSpec(memory_space=pltpu.MemorySpace.SMEM)
    V = pltpu.VMEM
    dma = lambda *shape: pltpu.SemaphoreType.DMA(shape) if shape else pltpu.SemaphoreType.DMA
    return pl.pallas_call(
        kernel,
        out_shape=jax.ShapeDtypeStruct((64, COLS), BF),
        in_specs=[smem, vmem, hbm, vmem, hbm, hbm, hbm, hbm, hbm, hbm, vmem, hbm, hbm, hbm],
        out_specs=vmem,
        scratch_shapes=[
            V((ROWS, MODEL_WIDTH), BF),
            V((ROWS, MODEL_WIDTH), BF),
            V((MODEL_WIDTH, HEADS * HD), BF),
            V((MODEL_WIDTH, HD), BF),
            V((MODEL_WIDTH, HD), BF),
            V((ROWS, SLOTS, HD), BF),
            V((ROWS, SLOTS, HD), BF),
            V((8 * ROWS, HD), F32),
            V((8 * ROWS, HD), F32),
            V((8 * ROWS, HD), F32),
            V((8 * ROWS, HD), F32),
            V((8 * ROWS, SLOTS), F32),
            V((8 * ROWS, SLOTS), F32),
            V((ROWS, HEADS * HD), BF),
            V((64, MODEL_WIDTH), BF),
            V((MODEL_WIDTH, COLS), BF),
            V((64, COLS), BF),
            V((2, COLS, 128), BF),
            V((2, COLS, 128), BF),
            V((4, COLS, 128), BF),
            V((2, 1024, CHUNK), BF),
            V((2, 512, 1024), BF),
            V((2, 4, 1, COLS), F32),
            V((2, 256, 1024), BF),
            V((64, COLS), F32),
            V((2, 256, CHUNK), BF),
            V((2, 4, 64, CHUNK), BF),
            V((2, 256, 512), BF),
            V((2, 256, 1024), BF),
            V((2, 4, 256, COLS), BF),
            V((256, COLS), F32),
            V((256, COLS), BF),
            V((4, 64, COLS), BF),
            V((256, 128), F32),
            V((2, 4, 8, 256), F32),
            V((256, COLS), BF),
            dma(11),
            dma(),
            dma(),
            dma(),
            dma(),
            dma(),
            dma(),
            dma(2, 3),
            dma(2, 4),
            dma(),
            dma(),
            pltpu.SemaphoreType.REGULAR,
            dma(),
            dma(4),
            dma(),
            dma(2, 4),
            dma(),
            dma(2, 4),
            dma(),
            dma(2, 4),
            dma(),
            dma(2, 4),
            dma(),
            dma(2, 4),
            dma(),
            dma(4),
            dma(),
            dma(),
            dma(),
            dma(),
        ],
        compiler_params=pltpu.CompilerParams(
            collective_id=0, has_side_effects=True, vmem_limit_bytes=56 << 20
        ),
    )(
        cache_lengths,
        positions.reshape(1, ROWS),
        residual_in,
        attn_gain.reshape(1, MODEL_WIDTH),
        query_weight,
        key_matrix,
        value_matrix,
        key_cache.reshape(ROWS, SLOTS, HD),
        cached_values.reshape(ROWS, SLOTS, HD),
        output_weight,
        mlp_gain.reshape(1, COLS),
        gate_weight,
        up_weight,
        down_weight,
    )


def solution(mesh):
    return jax.shard_map(
        shards,
        mesh=mesh,
        in_specs=(
            P(None, "req"),
            P(),
            P(None, "kv"),
            P(None, "kv"),
            P(None, "kv"),
            P("req", "kv", None, None),
            P("req", "kv", None, None),
            P("req"),
            P("req"),
            P(None, "req"),
            P("req"),
            P("req", "kv"),
            P("req", "kv"),
            P("kv", "req"),
        ),
        out_specs=P("kv", "req"),
        check_vma=False,
    )
```

```python
import functools
import math

import jax
import jax.numpy as jnp
from jax import lax
from jax.experimental import pallas as pl
from jax.experimental.pallas import tpu as pltpu
from jax.sharding import PartitionSpec as P

MODEL_WIDTH = 4096
WINDOW = 512
SINKS = 4
EPS = 1e-05
THETA = 10000.0

NR = 16
NK = 8
ROWS = 32
COLS = 256
HEADS = 4
HD = 128
SLOTS = 640
CHUNK = 896

BF = jnp.bfloat16
F32 = jnp.float32
MESH = pl.DeviceIdType.MESH
NT = (((1,), (1,)), ((), ()))
TN = (((0,), (0,)), ((), ()))


def dot(a, b):
    return jnp.dot(a, b, preferred_element_type=F32)


def piece_offset(l):
    return 448 * l + 64 * (l % 2)


def kernel(
    lens, pos, resid, gain1, wq, wk, wv, kc, vc, wo, gain2, gw, uw, dw,
    out,
    tok, nrm, wq_v, wk_v, wv_v, k_v, v_v, q3, k3, v3, o3, s3, w3, att, attb, wo_v, res_v,
    gp, up, pk, wp, dwp, gl, al, mid, pb, rf, hb, yb, yr, vf, fs, fb, invs, sqm, mb,
    ld, tokS, tokR, wS, wR, dS, dR, gS, gR, attS, attR, b2, yS, yR, lS, alR, sqS, sqR,
    rfS, rfR, hS, hR, oS, oR, fS, fR, swS, swR, sdS, sdR,
):
    r = lax.axis_index("req")
    k = lax.axis_index("kv")
    x, z = r // 4, r % 4
    y, c = k // 2, k % 2
    l = (1 - c) * x + c * z
    m = (1 - c) * z + c * x

    def dev(li, mi):
        return ((1 - c) * (4 * li + mi) + c * (4 * mi + li), k)

    def places(j):
        return (1 - j) * x + j * z, (1 - j) * z + j * x

    def devj(j, li, mi):
        return ((1 - j) * (4 * li + mi) + j * (4 * mi + li), k)

    sibling = (r, 2 * y + 1 - c)

    def rc(src, dst, ss, rs, to):
        return pltpu.make_async_remote_copy(
            src_ref=src, dst_ref=dst, send_sem=ss, recv_sem=rs, device_id=to, device_id_type=MESH
        )

    def arrived(ref, sem):
        pltpu.make_async_copy(ref, ref, sem).wait()

    def rows_of(i, n):
        return pl.ds(pl.multiple_of(n * i, n), n)

    barrier = pltpu.get_barrier_semaphore()
    for d in range(1, NR):
        pl.semaphore_signal(barrier, inc=1, device_id=((r + d) % NR, k), device_id_type=MESH)
    for d in range(1, NK):
        pl.semaphore_signal(barrier, inc=1, device_id=(r, (k + d) % NK), device_id_type=MESH)

    loads = {}

    def load(name, src, dst):
        loads[name] = pltpu.make_async_copy(src, dst, ld.at[len(loads)])
        loads[name].start()

    pltpu.make_async_copy(resid.at[rows_of(r, ROWS), :], tok.at[:, rows_of(r, COLS)], tokR).start()
    load("g3", gw.at[:, pl.ds(384, 128)], gp.at[0])
    load("g10", gw.at[:, pl.ds(1280, 128)], gp.at[1])
    load("u3", uw.at[:, pl.ds(384, 128)], up.at[0])
    load("u10", uw.at[:, pl.ds(1280, 128)], up.at[1])
    load("wq", wq, wq_v)
    load("wk", wk, wk_v)
    load("wv", wv, wv_v)

    pl.semaphore_wait(barrier, NR - 1 + NK - 1)

    for d in range(1, NR):
        to = (r + d) % NR
        rc(resid.at[rows_of(to, ROWS), :], tok.at[:, rows_of(r, COLS)], tokS, tokR, (to, k)).start()
    for d in range(1, NK):
        pl.semaphore_signal(b2, inc=1, device_id=(r, (k + d) % NK), device_id_type=MESH)

    load("kc", kc, k_v)

    def w_copies(d):
        to = (l + d) % 4
        off = pl.multiple_of(piece_offset(to), 128)
        here = rows_of(l, COLS)
        pieces = (
            (gw.at[:, pl.ds(off, 384)], wp.at[c, here, pl.ds(0, 384)]),
            (uw.at[:, pl.ds(off, 384)], wp.at[c, here, pl.ds(384, 384)]),
            (pk.at[to], wp.at[c, here, pl.ds(768, 128)]),
        )
        if d == 0:
            return [pltpu.make_async_copy(s, t, wR) for s, t in pieces]
        return [rc(s, t, wS, wR, dev(to, m)) for s, t in pieces]

    def d_copies(d):
        to = (l + d) % 4
        off = pl.multiple_of(piece_offset(to), 64)
        off2 = pl.multiple_of(384 + 896 * (to // 2) + 64 * (to % 2), 64)
        here = rows_of(l, COLS)
        pieces = (
            (dw.at[pl.ds(off, 384), :], dwp.at[c, pl.ds(0, 384), here]),
            (dw.at[pl.ds(off2, 64), :], dwp.at[c, pl.ds(384, 64), here]),
        )
        if d == 0:
            return [pltpu.make_async_copy(s, t, dR) for s, t in pieces]
        return [rc(s, t, dS, dR, dev(to, m)) for s, t in pieces]

    w_sends = {d: w_copies(d) for d in range(4)}
    for d in (1, 3, 2, 0):
        w_sends[d][0].start()
        w_sends[d][1].start()
    for name in ("g3", "g10", "u3", "u10"):
        loads[name].wait()
    low = lax.broadcasted_iota(jnp.int32, (COLS, 128), 1) < 64
    for t in range(2):
        g = gp[t].astype(F32)
        u = up[t].astype(F32)
        pk[2 * t] = jnp.where(low, g, pltpu.roll(u, 64, 1)).astype(BF)
        pk[2 * t + 1] = jnp.where(low, pltpu.roll(g, 64, 1), u).astype(BF)
    for d in (1, 3, 2, 0):
        w_sends[d][2].start()
    def gain_copies():
        out = []
        for j in range(2):
            lj, mj = places(j)
            for d in range(1, 4):
                to = devj(j, (lj + d) % 4, mj)
                out.append(rc(gain2, gl.at[j, lj], gS.at[j, d - 1], gR.at[j, lj], to))
        return out

    load("vc", vc, v_v)
    for j in range(2):
        gl[j, places(j)[0]] = gain2[...]
    for copy in gain_copies():
        copy.start()

    q3[...] = jnp.zeros_like(q3)
    k3[...] = jnp.zeros_like(k3)
    v3[...] = jnp.zeros_like(v3)
    for j in range(2):
        dwp[j, 448:512, :] = jnp.zeros((64, 1024), BF)

    load("wo", wo, wo_v)
    load("res", resid.at[rows_of(k, 64), :], res_v)

    sub = lax.broadcasted_iota(jnp.int32, (8, 128), 0)
    lane = lax.broadcasted_iota(jnp.int32, (ROWS, HD), 1)
    p8 = jnp.broadcast_to(pos[...].astype(F32), (8, ROWS))
    place = lax.dot_general(
        p8, (sub == 0).astype(F32), TN, preferred_element_type=F32, precision=lax.Precision.HIGHEST
    )
    freq = jnp.exp((lane % 64).astype(F32) * (-2.0 * math.log(THETA) / HD))
    angle = place * freq
    cs = jnp.cos(angle)
    sn = jnp.where(lane < 64, -1.0, 1.0) * jnp.sin(angle)

    arrived(tok, tokR)
    t = tok[...].astype(F32)
    scale = 1.0 / jnp.sqrt(jnp.sum(t * t, axis=-1, keepdims=True) / MODEL_WIDTH + EPS)
    nrm[...] = (t * scale * gain1[...]).astype(BF)
    loads["wq"].wait()
    loads["wk"].wait()
    loads["wv"].wait()
    q = dot(nrm[...], wq_v[...])
    kn = dot(nrm[...], wk_v[...])
    vn = dot(nrm[...], wv_v[...])

    def rotate(v):
        return (v * cs + pltpu.roll(v, 64, 1) * sn).astype(BF).astype(F32)

    kn = rotate(kn)
    vn = vn.astype(BF).astype(F32)
    for h in range(HEADS):
        q3[pl.ds(h, ROWS, stride=8), :] = rotate(q[:, HD * h : HD * (h + 1)])
        k3[pl.ds(h, ROWS, stride=8), :] = kn
        v3[pl.ds(h, ROWS, stride=8), :] = vn

    factor = 1.0 / math.sqrt(HD)
    slot = lax.broadcasted_iota(jnp.int32, (8, SLOTS), 1)
    loads["kc"].wait()
    kd = r // 2
    for half in range(2):
        for b in range(16 * half, 16 * half + 16):
            rows = slice(8 * b, 8 * b + 8)
            s = lax.dot_general(q3[rows, :].astype(BF), k_v[b], NT, preferred_element_type=F32)
            n = lens[b]
            ok = (slot < n) & ((slot < SINKS) | (slot > n - WINDOW))
            s3[rows, :] = jnp.where(ok, s * factor, -1e30)
        rows = slice(128 * half, 128 * half + 128)
        s = s3[rows, :]
        own = jnp.sum(q3[rows, :] * k3[rows, :], axis=-1, keepdims=True) * factor
        peak = jnp.maximum(jnp.max(s, axis=-1, keepdims=True), own)
        e = jnp.where(s > -1e29, jnp.exp(s - peak), 0.0)
        eo = jnp.exp(own - peak)
        inv = 1.0 / (jnp.sum(e, axis=-1, keepdims=True) + eo)
        w3[rows, :] = e * inv
        o3[rows, :] = (eo * inv).astype(BF).astype(F32) * v3[rows, :]
        if half == 0:
            loads["vc"].wait()
        for b in range(16 * half, 16 * half + 16):
            rows = slice(8 * b, 8 * b + 8)
            o3[rows, :] += dot(w3[rows, :].astype(BF), v_v[b])
        ours = slice(16 * half, 16 * half + 16)
        for h in range(HEADS):
            att[ours, HD * h : HD * (h + 1)] = o3[pl.ds(128 * half + h, 16, stride=8), :].astype(BF)

        block = att.at[ours, :]
        there = attb.at[pl.ds(pl.multiple_of(ROWS * (r % 2) + 16 * half, 16), 16), rows_of(k, 512)]
        if half == 0:
            pl.semaphore_wait(b2, NK - 1)

        @pl.when(k == kd)
        def _():
            pltpu.make_async_copy(block, there, attR).start()

        @pl.when(k != kd)
        def _():
            rc(block, there, attS, attR, (r, kd)).start()

        for d in range(1, NR):
            rc(block, there, attS, attR, ((r + d) % NR, kd)).start()

    arrived(tok.at[:, pl.ds(0, COLS * 15)], tokS)
    arrived(wp.at[c, pl.ds(0, 768), :], wS)
    for copy in gain_copies():
        copy.wait_send()

    loads["wo"].wait()
    loads["res"].wait()
    arrived(attb, attR)
    o = res_v[...].astype(F32) + dot(attb[...], wo_v[...])
    mid[...] = o
    mine = rows_of(y, 64)
    mb[mine, :] = (o * gain2[...]).astype(BF)

    around = (1, 3, 2)
    sets = (c, 1 - c)

    def line_sends(j, yp):
        lj, mj = places(j)
        at = rows_of(yp, 64)
        for e in around:
            rc(mb.at[at, :], al.at[j, at, rows_of(lj, COLS)], lS, alR.at[j, lj], devj(j, (lj + e) % 4, mj)).start()

    for e in around:
        rc(mb.at[mine, :], mb.at[mine, :], yS, yR.at[y], (r, 2 * ((y + e) % 4) + c)).start()
    for j in sets:
        line_sends(j, y)
    for i, j in enumerate(sets):
        for e in around:
            yp = (y + e) % 4
            if i == 0:
                arrived(mb.at[rows_of(yp, 64), :], yR.at[yp])
            line_sends(j, yp)
    arrived(wp.at[c], wR)
    rc(wp.at[c], wp.at[c], swS, swR, sibling).start()
    for d in (1, 3, 2, 0):
        for copy in d_copies(d):
            copy.start()
    for j in range(2):
        al[j, :, rows_of(places(j)[0], COLS)] = mb[...]

    @pl.when(k == kd)
    def _():
        arrived(attb.at[pl.ds(0, 32), pl.ds(0, 3584)], attS)
        arrived(attb.at[pl.ds(32, 32), pl.ds(0, 4096)], attS)

    @pl.when(k != kd)
    def _():
        arrived(attb, attS)

    def silu(v):
        return v / (1.0 + jnp.exp(-v))

    def gate(j):
        lj, mj = places(j)
        for e in around:
            lp = (lj + e) % 4
            arrived(al.at[j, :, rows_of(lp, COLS)], alR.at[j, lp])
        pb[j] = dot(al[j], wp[j]).astype(BF)
        for e in around:
            mi = (mj + e) % 4
            rc(pb.at[j, rows_of(mi, 64), :], rf.at[j, mj], rfS, rfR.at[j, mj], devj(j, lj, mi)).start()
        for e in around:
            at = (lj + e) % 4
            arrived(gl.at[j, at], gR.at[j, at])
        part = jnp.zeros((256, 128), F32)
        for i in range(8):
            g = 1.0 / gl[j, i // 2, :, 128 * (i % 2) : 128 * (i % 2) + 128]
            v = al[j, :, 128 * i : 128 * (i + 1)].astype(F32) * g
            part = part + v * v
        sqm[j, mj] = lax.dot_general(
            jnp.ones((8, 128), F32), part, NT, preferred_element_type=F32, precision=lax.Precision.HIGHEST
        )
        for e in around:
            mi = (mj + e) % 4
            rc(sqm.at[j, mj], sqm.at[j, mj], sqS, sqR.at[j, mj], devj(j, lj, mi)).start()

    def hide(j):
        lj, mj = places(j)
        here = rows_of(mj, 64)
        for e in around:
            mi = (mj + e) % 4
            arrived(sqm.at[j, mi], sqR.at[j, mi])
        total = lax.dot_general(
            sqm[j, 0] + sqm[j, 1] + sqm[j, 2] + sqm[j, 3],
            (sub == 0).astype(F32),
            TN,
            preferred_element_type=F32,
            precision=lax.Precision.HIGHEST,
        )
        invs[...] = 1.0 / jnp.sqrt(total / MODEL_WIDTH + EPS)
        inv = invs[here, :]
        for e in around:
            mi = (mj + e) % 4
            arrived(rf.at[j, mi], rfR.at[j, mi])

        def tile(i):
            at = slice(128 * i, 128 * (i + 1))
            v = pb[j, here, at].astype(F32)
            for e in around:
                v = v + rf[j, (mj + e) % 4, :, at].astype(F32)
            return v * inv

        for i in range(3):
            hb[j, here, 128 * i : 128 * (i + 1)] = (silu(tile(i)) * tile(3 + i)).astype(BF)
        t = tile(6)
        low = lax.broadcasted_iota(jnp.int32, (64, 128), 1) < 64
        hb[j, here, 384:512] = jnp.where(low, silu(t) * pltpu.roll(t, 64, 1), 0.0).astype(BF)
        for e in around:
            rc(hb.at[j, here, :], hb.at[j, here, :], hS, hR.at[j, mj], devj(j, lj, (mj + e) % 4)).start()

    gate(c)
    arrived(wp.at[1 - c], swR)
    gate(1 - c)
    arrived(dwp.at[c, pl.ds(0, 448), :], dR)
    rc(dwp.at[c, pl.ds(0, 448), :], dwp.at[c, pl.ds(0, 448), :], sdS, sdR, sibling).start()
    for j in sets:
        hide(j)

    arrived(wp.at[c], swS)
    arrived(mb.at[pl.ds(0, 192), :], yS)
    arrived(al.at[:, :, pl.ds(0, 768)], lS)
    arrived(pb.at[:, pl.ds(0, 192), :], rfS)
    arrived(sqm.at[:, pl.ds(0, 3)], sqS)
    arrived(dwp.at[c, pl.ds(0, 448), pl.ds(0, 768)], dS)

    def down(j):
        lj, mj = places(j)
        for e in around:
            mi = (mj + e) % 4
            arrived(hb.at[j, rows_of(mi, 64), :], hR.at[j, mi])
        yb[j] = dot(hb[j], dwp[j]).astype(BF)
        for e in around:
            to = (lj + e) % 4
            rc(yb.at[j, :, rows_of(to, COLS)], yr.at[j, lj], oS, oR.at[j, lj], devj(j, to, mj)).start()

    down(c)
    arrived(dwp.at[1 - c, pl.ds(0, 448), :], sdR)
    down(1 - c)
    v = jnp.zeros((256, COLS), F32)
    for j in sets:
        lj, mj = places(j)
        v = v + yb[j, :, rows_of(lj, COLS)].astype(F32)
        for e in around:
            lp = (lj + e) % 4
            arrived(yr.at[j, lp], oR.at[j, lp])
            v = v + yr[j, lp].astype(F32)
    vf[...] = v
    fs[...] = v.astype(BF)
    for e in around:
        yp = (y + e) % 4
        rc(fs.at[rows_of(yp, 64), :], fb.at[y], fS, fR.at[y], (r, 2 * yp + c)).start()
    arrived(hb.at[:, pl.ds(0, 192), :], hS)
    arrived(yb.at[:, :, pl.ds(0, 768)], oS)
    arrived(dwp.at[c, pl.ds(0, 448), :], sdS)
    res = mid[...] + vf[mine, :]
    for e in around:
        yp = (y + e) % 4
        arrived(fb.at[yp], fR.at[yp])
        res = res + fb[yp].astype(F32)
    out[...] = res.astype(BF)
    arrived(fs.at[pl.ds(0, 192), :], fS)


def shards(
    residual_in,
    attn_gain,
    query_weight,
    key_matrix,
    value_matrix,
    key_cache,
    cached_values,
    cache_lengths,
    positions,
    output_weight,
    mlp_gain,
    gate_weight,
    up_weight,
    down_weight,
):
    hbm = pl.BlockSpec(memory_space=pltpu.MemorySpace.HBM)
    vmem = pl.BlockSpec(memory_space=pltpu.MemorySpace.VMEM)
    smem = pl.BlockSpec(memory_space=pltpu.MemorySpace.SMEM)
    V = pltpu.VMEM
    dma = lambda *shape: pltpu.SemaphoreType.DMA(shape) if shape else pltpu.SemaphoreType.DMA
    return pl.pallas_call(
        kernel,
        out_shape=jax.ShapeDtypeStruct((64, COLS), BF),
        in_specs=[smem, vmem, hbm, vmem, hbm, hbm, hbm, hbm, hbm, hbm, vmem, hbm, hbm, hbm],
        out_specs=vmem,
        scratch_shapes=[
            V((ROWS, MODEL_WIDTH), BF),
            V((ROWS, MODEL_WIDTH), BF),
            V((MODEL_WIDTH, HEADS * HD), BF),
            V((MODEL_WIDTH, HD), BF),
            V((MODEL_WIDTH, HD), BF),
            V((ROWS, SLOTS, HD), BF),
            V((ROWS, SLOTS, HD), BF),
            V((8 * ROWS, HD), F32),
            V((8 * ROWS, HD), F32),
            V((8 * ROWS, HD), F32),
            V((8 * ROWS, HD), F32),
            V((8 * ROWS, SLOTS), F32),
            V((8 * ROWS, SLOTS), F32),
            V((ROWS, HEADS * HD), BF),
            V((64, MODEL_WIDTH), BF),
            V((MODEL_WIDTH, COLS), BF),
            V((64, COLS), BF),
            V((2, COLS, 128), BF),
            V((2, COLS, 128), BF),
            V((4, COLS, 128), BF),
            V((2, 1024, CHUNK), BF),
            V((2, 512, 1024), BF),
            V((2, 4, 1, COLS), F32),
            V((2, 256, 1024), BF),
            V((64, COLS), F32),
            V((2, 256, CHUNK), BF),
            V((2, 4, 64, CHUNK), BF),
            V((2, 256, 512), BF),
            V((2, 256, 1024), BF),
            V((2, 4, 256, COLS), BF),
            V((256, COLS), F32),
            V((256, COLS), BF),
            V((4, 64, COLS), BF),
            V((256, 128), F32),
            V((2, 4, 8, 256), F32),
            V((256, COLS), BF),
            dma(11),
            dma(),
            dma(),
            dma(),
            dma(),
            dma(),
            dma(),
            dma(2, 3),
            dma(2, 4),
            dma(),
            dma(),
            pltpu.SemaphoreType.REGULAR,
            dma(),
            dma(4),
            dma(),
            dma(2, 4),
            dma(),
            dma(2, 4),
            dma(),
            dma(2, 4),
            dma(),
            dma(2, 4),
            dma(),
            dma(2, 4),
            dma(),
            dma(4),
            dma(),
            dma(),
            dma(),
            dma(),
        ],
        compiler_params=pltpu.CompilerParams(
            collective_id=0, has_side_effects=True, vmem_limit_bytes=56 << 20
        ),
    )(
        cache_lengths,
        positions.reshape(1, ROWS),
        residual_in,
        attn_gain.reshape(1, MODEL_WIDTH),
        query_weight,
        key_matrix,
        value_matrix,
        key_cache.reshape(ROWS, SLOTS, HD),
        cached_values.reshape(ROWS, SLOTS, HD),
        output_weight,
        mlp_gain.reshape(1, COLS),
        gate_weight,
        up_weight,
        down_weight,
    )


def solution(mesh):
    return jax.shard_map(
        shards,
        mesh=mesh,
        in_specs=(
            P(None, "req"),
            P(),
            P(None, "kv"),
            P(None, "kv"),
            P(None, "kv"),
            P("req", "kv", None, None),
            P("req", "kv", None, None),
            P("req"),
            P("req"),
            P(None, "req"),
            P("req"),
            P("req", "kv"),
            P("req", "kv"),
            P("kv", "req"),
        ),
        out_specs=P("kv", "req"),
        check_vma=False,
    )
```

```python
import functools
import math

import jax
import jax.numpy as jnp
from jax import lax
from jax.experimental import pallas as pl
from jax.experimental.pallas import tpu as pltpu
from jax.sharding import PartitionSpec as P

MODEL_WIDTH = 4096
WINDOW = 512
SINKS = 4
EPS = 1e-05
THETA = 10000.0

NR = 16
NK = 8
ROWS = 32
COLS = 256
HEADS = 4
HD = 128
SLOTS = 640
CHUNK = 896

BF = jnp.bfloat16
F32 = jnp.float32
MESH = pl.DeviceIdType.MESH
NT = (((1,), (1,)), ((), ()))
TN = (((0,), (0,)), ((), ()))


def dot(a, b):
    return jnp.dot(a, b, preferred_element_type=F32)


def piece_offset(l):
    return 448 * l + 64 * (l % 2)


def kernel(
    lens_h, pos_h, resid, gain1_h, wq, wk, wv, kc, vc, wo, gain2_h, gw, uw, dw,
    out,
    lens, pos, gain1, gain2,
    tok, nrm, wq_v, wk_v, wv_v, k_v, v_v, q3, k3, v3, o3, s3, w3, att, attb, wo_v, res_v,
    gp, up, pk, wp, dwp, gl, al, mid, pb, rf, hb, yb, yr, vf, fs, fb, invs, sqm, mb,
    ld, tokS, tokR, wS, wR, dS, dR, gS, gR, attS, attR, b2, yS, yR, lS, alR, sqS, sqR,
    rfS, rfR, hS, hR, oS, oR, fS, fR, swS, swR, sdS, sdR,
):
    r = lax.axis_index("req")
    k = lax.axis_index("kv")
    x, z = r // 4, r % 4
    y, c = k // 2, k % 2
    l = (1 - c) * x + c * z
    m = (1 - c) * z + c * x

    def dev(li, mi):
        return ((1 - c) * (4 * li + mi) + c * (4 * mi + li), k)

    def places(j):
        return (1 - j) * x + j * z, (1 - j) * z + j * x

    def devj(j, li, mi):
        return ((1 - j) * (4 * li + mi) + j * (4 * mi + li), k)

    sibling = (r, 2 * y + 1 - c)

    def rc(src, dst, ss, rs, to):
        return pltpu.make_async_remote_copy(
            src_ref=src, dst_ref=dst, send_sem=ss, recv_sem=rs, device_id=to, device_id_type=MESH
        )

    def arrived(ref, sem):
        pltpu.make_async_copy(ref, ref, sem).wait()

    def rows_of(i, n):
        return pl.ds(pl.multiple_of(n * i, n), n)

    barrier = pltpu.get_barrier_semaphore()
    for d in range(1, NR):
        pl.semaphore_signal(barrier, inc=1, device_id=((r + d) % NR, k), device_id_type=MESH)
    for d in range(1, NK):
        pl.semaphore_signal(barrier, inc=1, device_id=(r, (k + d) % NK), device_id_type=MESH)

    loads = {}

    def load(name, src, dst):
        loads[name] = pltpu.make_async_copy(src, dst, ld.at[len(loads)])
        loads[name].start()

    pltpu.make_async_copy(resid.at[rows_of(r, ROWS), :], tok.at[:, rows_of(r, COLS)], tokR).start()
    load("g3", gw.at[:, pl.ds(384, 128)], gp.at[0])
    load("g10", gw.at[:, pl.ds(1280, 128)], gp.at[1])
    load("u3", uw.at[:, pl.ds(384, 128)], up.at[0])
    load("u10", uw.at[:, pl.ds(1280, 128)], up.at[1])
    load("gain2", gain2_h, gain2)
    load("gain1", gain1_h, gain1)
    load("lens", lens_h, lens)
    load("pos", pos_h, pos)
    load("wq", wq, wq_v)
    load("wk", wk, wk_v)
    load("wv", wv, wv_v)

    pl.semaphore_wait(barrier, NR - 1 + NK - 1)

    for d in range(1, NR):
        to = (r + d) % NR
        rc(resid.at[rows_of(to, ROWS), :], tok.at[:, rows_of(r, COLS)], tokS, tokR, (to, k)).start()
    for d in range(1, NK):
        pl.semaphore_signal(b2, inc=1, device_id=(r, (k + d) % NK), device_id_type=MESH)

    load("kc", kc, k_v)

    def w_copies(d):
        to = (l + d) % 4
        off = pl.multiple_of(piece_offset(to), 128)
        here = rows_of(l, COLS)
        pieces = (
            (gw.at[:, pl.ds(off, 384)], wp.at[c, here, pl.ds(0, 384)]),
            (uw.at[:, pl.ds(off, 384)], wp.at[c, here, pl.ds(384, 384)]),
            (pk.at[to], wp.at[c, here, pl.ds(768, 128)]),
        )
        if d == 0:
            return [pltpu.make_async_copy(s, t, wR) for s, t in pieces]
        return [rc(s, t, wS, wR, dev(to, m)) for s, t in pieces]

    def d_copies(d):
        to = (l + d) % 4
        off = pl.multiple_of(piece_offset(to), 64)
        off2 = pl.multiple_of(384 + 896 * (to // 2) + 64 * (to % 2), 64)
        here = rows_of(l, COLS)
        pieces = (
            (dw.at[pl.ds(off, 384), :], dwp.at[c, pl.ds(0, 384), here]),
            (dw.at[pl.ds(off2, 64), :], dwp.at[c, pl.ds(384, 64), here]),
        )
        if d == 0:
            return [pltpu.make_async_copy(s, t, dR) for s, t in pieces]
        return [rc(s, t, dS, dR, dev(to, m)) for s, t in pieces]

    w_sends = {d: w_copies(d) for d in range(4)}
    for d in (1, 3, 2, 0):
        w_sends[d][0].start()
        w_sends[d][1].start()
    for name in ("g3", "g10", "u3", "u10"):
        loads[name].wait()
    low = lax.broadcasted_iota(jnp.int32, (COLS, 128), 1) < 64
    for t in range(2):
        g = gp[t].astype(F32)
        u = up[t].astype(F32)
        pk[2 * t] = jnp.where(low, g, pltpu.roll(u, 64, 1)).astype(BF)
        pk[2 * t + 1] = jnp.where(low, pltpu.roll(g, 64, 1), u).astype(BF)
    for d in (1, 3, 2, 0):
        w_sends[d][2].start()
    def gain_copies():
        out = []
        for j in range(2):
            lj, mj = places(j)
            for d in range(1, 4):
                to = devj(j, (lj + d) % 4, mj)
                out.append(rc(gain2, gl.at[j, lj], gS.at[j, d - 1], gR.at[j, lj], to))
        return out

    load("vc", vc, v_v)
    loads["gain2"].wait()
    for j in range(2):
        gl[j, places(j)[0]] = gain2[...]
    for copy in gain_copies():
        copy.start()

    q3[...] = jnp.zeros_like(q3)
    k3[...] = jnp.zeros_like(k3)
    v3[...] = jnp.zeros_like(v3)
    for j in range(2):
        dwp[j, 448:512, :] = jnp.zeros((64, 1024), BF)

    load("wo", wo, wo_v)
    load("res", resid.at[rows_of(k, 64), :], res_v)

    loads["pos"].wait()
    loads["lens"].wait()
    loads["gain1"].wait()
    sub = lax.broadcasted_iota(jnp.int32, (8, 128), 0)
    lane = lax.broadcasted_iota(jnp.int32, (ROWS, HD), 1)
    p8 = jnp.broadcast_to(pos[...].astype(F32), (8, ROWS))
    place = lax.dot_general(
        p8, (sub == 0).astype(F32), TN, preferred_element_type=F32, precision=lax.Precision.HIGHEST
    )
    freq = jnp.exp((lane % 64).astype(F32) * (-2.0 * math.log(THETA) / HD))
    angle = place * freq
    cs = jnp.cos(angle)
    sn = jnp.where(lane < 64, -1.0, 1.0) * jnp.sin(angle)

    arrived(tok, tokR)
    t = tok[...].astype(F32)
    scale = 1.0 / jnp.sqrt(jnp.sum(t * t, axis=-1, keepdims=True) / MODEL_WIDTH + EPS)
    nrm[...] = (t * scale * gain1[...]).astype(BF)
    loads["wq"].wait()
    loads["wk"].wait()
    loads["wv"].wait()
    q = dot(nrm[...], wq_v[...])
    kn = dot(nrm[...], wk_v[...])
    vn = dot(nrm[...], wv_v[...])

    def rotate(v):
        return (v * cs + pltpu.roll(v, 64, 1) * sn).astype(BF).astype(F32)

    kn = rotate(kn)
    vn = vn.astype(BF).astype(F32)
    for h in range(HEADS):
        q3[pl.ds(h, ROWS, stride=8), :] = rotate(q[:, HD * h : HD * (h + 1)])
        k3[pl.ds(h, ROWS, stride=8), :] = kn
        v3[pl.ds(h, ROWS, stride=8), :] = vn

    factor = 1.0 / math.sqrt(HD)
    slot = lax.broadcasted_iota(jnp.int32, (8, SLOTS), 1)
    loads["kc"].wait()
    kd = r // 2
    for half in range(2):
        for b in range(16 * half, 16 * half + 16):
            rows = slice(8 * b, 8 * b + 8)
            s = lax.dot_general(q3[rows, :].astype(BF), k_v[b], NT, preferred_element_type=F32)
            n = lens[0, b]
            ok = (slot < n) & ((slot < SINKS) | (slot > n - WINDOW))
            s3[rows, :] = jnp.where(ok, s * factor, -1e30)
        rows = slice(128 * half, 128 * half + 128)
        s = s3[rows, :]
        own = jnp.sum(q3[rows, :] * k3[rows, :], axis=-1, keepdims=True) * factor
        peak = jnp.maximum(jnp.max(s, axis=-1, keepdims=True), own)
        e = jnp.where(s > -1e29, jnp.exp(s - peak), 0.0)
        eo = jnp.exp(own - peak)
        inv = 1.0 / (jnp.sum(e, axis=-1, keepdims=True) + eo)
        w3[rows, :] = e * inv
        o3[rows, :] = (eo * inv).astype(BF).astype(F32) * v3[rows, :]
        if half == 0:
            loads["vc"].wait()
        for b in range(16 * half, 16 * half + 16):
            rows = slice(8 * b, 8 * b + 8)
            o3[rows, :] += dot(w3[rows, :].astype(BF), v_v[b])
        ours = slice(16 * half, 16 * half + 16)
        for h in range(HEADS):
            att[ours, HD * h : HD * (h + 1)] = o3[pl.ds(128 * half + h, 16, stride=8), :].astype(BF)

        block = att.at[ours, :]
        there = attb.at[pl.ds(pl.multiple_of(ROWS * (r % 2) + 16 * half, 16), 16), rows_of(k, 512)]
        if half == 0:
            pl.semaphore_wait(b2, NK - 1)

        @pl.when(k == kd)
        def _():
            pltpu.make_async_copy(block, there, attR.at[k]).start()

        @pl.when(k != kd)
        def _():
            rc(block, there, attS, attR.at[k], (r, kd)).start()

        for d in range(1, NR):
            rc(block, there, attS, attR.at[k], ((r + d) % NR, kd)).start()

    arrived(tok.at[:, pl.ds(0, COLS * 15)], tokS)
    arrived(wp.at[c, pl.ds(0, 768), :], wS)
    for copy in gain_copies():
        copy.wait_send()

    loads["wo"].wait()
    loads["res"].wait()
    o = res_v[...].astype(F32)
    for d in (0, 1, 2, 3, 6, 7, 4, 5):
        kp = 2 * ((y + d // 2) % 4) + (c + d % 2) % 2
        arrived(attb.at[:, rows_of(kp, 512)], attR.at[kp])
        o = o + dot(attb[:, rows_of(kp, 512)], wo_v[rows_of(kp, 512), :])
    mid[...] = o
    mine = rows_of(y, 64)
    mb[mine, :] = (o * gain2[...]).astype(BF)

    around = (2, 1, 3)
    sets = (c, 1 - c)

    def line_sends(j, yp):
        lj, mj = places(j)
        at = rows_of(yp, 64)
        for e in around:
            rc(mb.at[at, :], al.at[j, at, rows_of(lj, COLS)], lS, alR.at[j, lj], devj(j, (lj + e) % 4, mj)).start()

    for e in around:
        rc(mb.at[mine, :], mb.at[mine, :], yS, yR.at[y], (r, 2 * ((y + e) % 4) + c)).start()
    for j in sets:
        line_sends(j, y)
    for i, j in enumerate(sets):
        for e in around:
            yp = (y + e) % 4
            if i == 0:
                arrived(mb.at[rows_of(yp, 64), :], yR.at[yp])
            line_sends(j, yp)
    arrived(wp.at[c], wR)
    rc(wp.at[c], wp.at[c], swS, swR, sibling).start()
    for d in (1, 3, 2, 0):
        for copy in d_copies(d):
            copy.start()
    for j in range(2):
        al[j, :, rows_of(places(j)[0], COLS)] = mb[...]

    @pl.when(k == kd)
    def _():
        arrived(attb.at[pl.ds(0, 32), pl.ds(0, 3584)], attS)
        arrived(attb.at[pl.ds(32, 32), pl.ds(0, 4096)], attS)

    @pl.when(k != kd)
    def _():
        arrived(attb, attS)

    def silu(v):
        return v / (1.0 + jnp.exp(-v))

    def gate(j):
        lj, mj = places(j)
        for e in around:
            lp = (lj + e) % 4
            arrived(al.at[j, :, rows_of(lp, COLS)], alR.at[j, lp])
        pb[j] = dot(al[j], wp[j]).astype(BF)
        for e in around:
            mi = (mj + e) % 4
            rc(pb.at[j, rows_of(mi, 64), :], rf.at[j, mj], rfS, rfR.at[j, mj], devj(j, lj, mi)).start()
        for e in around:
            at = (lj + e) % 4
            arrived(gl.at[j, at], gR.at[j, at])
        part = jnp.zeros((256, 128), F32)
        for i in range(8):
            g = 1.0 / gl[j, i // 2, :, 128 * (i % 2) : 128 * (i % 2) + 128]
            v = al[j, :, 128 * i : 128 * (i + 1)].astype(F32) * g
            part = part + v * v
        sqm[j, mj] = lax.dot_general(
            jnp.ones((8, 128), F32), part, NT, preferred_element_type=F32, precision=lax.Precision.HIGHEST
        )
        for e in around:
            mi = (mj + e) % 4
            rc(sqm.at[j, mj], sqm.at[j, mj], sqS, sqR.at[j, mj], devj(j, lj, mi)).start()

    def hide(j):
        lj, mj = places(j)
        here = rows_of(mj, 64)
        for e in around:
            mi = (mj + e) % 4
            arrived(sqm.at[j, mi], sqR.at[j, mi])
        total = lax.dot_general(
            sqm[j, 0] + sqm[j, 1] + sqm[j, 2] + sqm[j, 3],
            (sub == 0).astype(F32),
            TN,
            preferred_element_type=F32,
            precision=lax.Precision.HIGHEST,
        )
        invs[...] = 1.0 / jnp.sqrt(total / MODEL_WIDTH + EPS)
        inv = invs[here, :]
        for e in around:
            mi = (mj + e) % 4
            arrived(rf.at[j, mi], rfR.at[j, mi])

        def tile(i):
            at = slice(128 * i, 128 * (i + 1))
            v = pb[j, here, at].astype(F32)
            for e in around:
                v = v + rf[j, (mj + e) % 4, :, at].astype(F32)
            return v * inv

        for i in range(3):
            hb[j, here, 128 * i : 128 * (i + 1)] = (silu(tile(i)) * tile(3 + i)).astype(BF)
        t = tile(6)
        low = lax.broadcasted_iota(jnp.int32, (64, 128), 1) < 64
        hb[j, here, 384:512] = jnp.where(low, silu(t) * pltpu.roll(t, 64, 1), 0.0).astype(BF)
        for e in around:
            rc(hb.at[j, here, :], hb.at[j, here, :], hS, hR.at[j, mj], devj(j, lj, (mj + e) % 4)).start()

    gate(c)
    arrived(wp.at[1 - c], swR)
    gate(1 - c)
    arrived(dwp.at[c, pl.ds(0, 448), :], dR)
    rc(dwp.at[c, pl.ds(0, 448), :], dwp.at[c, pl.ds(0, 448), :], sdS, sdR, sibling).start()
    for j in sets:
        hide(j)

    arrived(wp.at[c], swS)
    arrived(mb.at[pl.ds(0, 192), :], yS)
    arrived(al.at[:, :, pl.ds(0, 768)], lS)
    arrived(pb.at[:, pl.ds(0, 192), :], rfS)
    arrived(sqm.at[:, pl.ds(0, 3)], sqS)
    arrived(dwp.at[c, pl.ds(0, 448), pl.ds(0, 768)], dS)

    def down(j):
        lj, mj = places(j)
        for e in around:
            mi = (mj + e) % 4
            arrived(hb.at[j, rows_of(mi, 64), :], hR.at[j, mi])
        yb[j] = dot(hb[j], dwp[j]).astype(BF)
        for e in around:
            to = (lj + e) % 4
            rc(yb.at[j, :, rows_of(to, COLS)], yr.at[j, lj], oS, oR.at[j, lj], devj(j, to, mj)).start()

    down(c)
    arrived(dwp.at[1 - c, pl.ds(0, 448), :], sdR)
    down(1 - c)
    v = jnp.zeros((256, COLS), F32)
    for j in sets:
        lj, mj = places(j)
        v = v + yb[j, :, rows_of(lj, COLS)].astype(F32)
        for e in around:
            lp = (lj + e) % 4
            arrived(yr.at[j, lp], oR.at[j, lp])
            v = v + yr[j, lp].astype(F32)
    vf[...] = v
    fs[...] = v.astype(BF)
    for e in around:
        yp = (y + e) % 4
        rc(fs.at[rows_of(yp, 64), :], fb.at[y], fS, fR.at[y], (r, 2 * yp + c)).start()
    arrived(hb.at[:, pl.ds(0, 192), :], hS)
    arrived(yb.at[:, :, pl.ds(0, 768)], oS)
    arrived(dwp.at[c, pl.ds(0, 448), :], sdS)
    res = mid[...] + vf[mine, :]
    for e in around:
        yp = (y + e) % 4
        arrived(fb.at[yp], fR.at[yp])
        res = res + fb[yp].astype(F32)
    out[...] = res.astype(BF)
    arrived(fs.at[pl.ds(0, 192), :], fS)


def shards(
    residual_in,
    attn_gain,
    query_weight,
    key_matrix,
    value_matrix,
    key_cache,
    cached_values,
    cache_lengths,
    positions,
    output_weight,
    mlp_gain,
    gate_weight,
    up_weight,
    down_weight,
):
    hbm = pl.BlockSpec(memory_space=pltpu.MemorySpace.HBM)
    vmem = pl.BlockSpec(memory_space=pltpu.MemorySpace.VMEM)
    V = pltpu.VMEM
    dma = lambda *shape: pltpu.SemaphoreType.DMA(shape) if shape else pltpu.SemaphoreType.DMA
    return pl.pallas_call(
        kernel,
        out_shape=jax.ShapeDtypeStruct((64, COLS), BF),
        in_specs=[hbm] * 14,
        out_specs=vmem,
        scratch_shapes=[
            pltpu.SMEM((1, ROWS), jnp.int32),
            V((1, ROWS), jnp.int32),
            V((1, MODEL_WIDTH), F32),
            V((1, COLS), F32),
            V((ROWS, MODEL_WIDTH), BF),
            V((ROWS, MODEL_WIDTH), BF),
            V((MODEL_WIDTH, HEADS * HD), BF),
            V((MODEL_WIDTH, HD), BF),
            V((MODEL_WIDTH, HD), BF),
            V((ROWS, SLOTS, HD), BF),
            V((ROWS, SLOTS, HD), BF),
            V((8 * ROWS, HD), F32),
            V((8 * ROWS, HD), F32),
            V((8 * ROWS, HD), F32),
            V((8 * ROWS, HD), F32),
            V((8 * ROWS, SLOTS), F32),
            V((8 * ROWS, SLOTS), F32),
            V((ROWS, HEADS * HD), BF),
            V((64, MODEL_WIDTH), BF),
            V((MODEL_WIDTH, COLS), BF),
            V((64, COLS), BF),
            V((2, COLS, 128), BF),
            V((2, COLS, 128), BF),
            V((4, COLS, 128), BF),
            V((2, 1024, CHUNK), BF),
            V((2, 512, 1024), BF),
            V((2, 4, 1, COLS), F32),
            V((2, 256, 1024), BF),
            V((64, COLS), F32),
            V((2, 256, CHUNK), BF),
            V((2, 4, 64, CHUNK), BF),
            V((2, 256, 512), BF),
            V((2, 256, 1024), BF),
            V((2, 4, 256, COLS), BF),
            V((256, COLS), F32),
            V((256, COLS), BF),
            V((4, 64, COLS), BF),
            V((256, 128), F32),
            V((2, 4, 8, 256), F32),
            V((256, COLS), BF),
            dma(15),
            dma(),
            dma(),
            dma(),
            dma(),
            dma(),
            dma(),
            dma(2, 3),
            dma(2, 4),
            dma(),
            dma(NK),
            pltpu.SemaphoreType.REGULAR,
            dma(),
            dma(4),
            dma(),
            dma(2, 4),
            dma(),
            dma(2, 4),
            dma(),
            dma(2, 4),
            dma(),
            dma(2, 4),
            dma(),
            dma(2, 4),
            dma(),
            dma(4),
            dma(),
            dma(),
            dma(),
            dma(),
        ],
        compiler_params=pltpu.CompilerParams(
            collective_id=0, has_side_effects=True, vmem_limit_bytes=56 << 20
        ),
    )(
        cache_lengths.reshape(1, ROWS),
        positions.reshape(1, ROWS),
        residual_in,
        attn_gain.reshape(1, MODEL_WIDTH),
        query_weight,
        key_matrix,
        value_matrix,
        key_cache.reshape(ROWS, SLOTS, HD),
        cached_values.reshape(ROWS, SLOTS, HD),
        output_weight,
        mlp_gain.reshape(1, COLS),
        gate_weight,
        up_weight,
        down_weight,
    )


def solution(mesh):
    return jax.shard_map(
        shards,
        mesh=mesh,
        in_specs=(
            P(None, "req"),
            P(),
            P(None, "kv"),
            P(None, "kv"),
            P(None, "kv"),
            P("req", "kv", None, None),
            P("req", "kv", None, None),
            P("req"),
            P("req"),
            P(None, "req"),
            P("req"),
            P("req", "kv"),
            P("req", "kv"),
            P("kv", "req"),
        ),
        out_specs=P("kv", "req"),
        check_vma=False,
    )
```

```python
import functools
import math

import jax
import jax.numpy as jnp
from jax import lax
from jax.experimental import pallas as pl
from jax.experimental.pallas import tpu as pltpu
from jax.sharding import PartitionSpec as P

MODEL_WIDTH = 4096
WINDOW = 512
SINKS = 4
EPS = 1e-05
THETA = 10000.0

NR = 16
NK = 8
ROWS = 32
COLS = 256
HEADS = 4
HD = 128
SLOTS = 640
CHUNK = 896

BF = jnp.bfloat16
F32 = jnp.float32
MESH = pl.DeviceIdType.MESH
NT = (((1,), (1,)), ((), ()))
TN = (((0,), (0,)), ((), ()))


def dot(a, b):
    return jnp.dot(a, b, preferred_element_type=F32)


def piece_offset(l):
    return 448 * l + 64 * (l % 2)


def kernel(
    lens_h, pos_h, resid, gain1_h, wq, wk, wv, kc, vc, wo, gain2_h, gw, uw, dw,
    out,
    lens, pos, gain1, gain2,
    tok, nrm, wq_v, wk_v, wv_v, k_v, v_v, q3, k3, v3, o3, s3, w3, att, attb, wo_v, res_v,
    gp, up, pk, wp, dwp, gl, al, mid, pb, rf, hb, yb, yr, vf, fs, fb, invs, sqm, mb,
    ld, tokS, tokR, wS, wR, dS, dR, gS, gR, attS, attR, b2, yS, yR, lS, alR, sqS, sqR,
    rfS, rfR, hS, hR, oS, oR, fS, fR, swS, swR, sdS, sdR,
):
    r = lax.axis_index("req")
    k = lax.axis_index("kv")
    x, z = r // 4, r % 4
    y, c = k // 2, k % 2
    l = (1 - c) * x + c * z
    m = (1 - c) * z + c * x

    def dev(li, mi):
        return ((1 - c) * (4 * li + mi) + c * (4 * mi + li), k)

    def places(j):
        return (1 - j) * x + j * z, (1 - j) * z + j * x

    def devj(j, li, mi):
        return ((1 - j) * (4 * li + mi) + j * (4 * mi + li), k)

    sibling = (r, 2 * y + 1 - c)

    def rc(src, dst, ss, rs, to):
        return pltpu.make_async_remote_copy(
            src_ref=src, dst_ref=dst, send_sem=ss, recv_sem=rs, device_id=to, device_id_type=MESH
        )

    def arrived(ref, sem):
        pltpu.make_async_copy(ref, ref, sem).wait()

    def rows_of(i, n):
        return pl.ds(pl.multiple_of(n * i, n), n)

    barrier = pltpu.get_barrier_semaphore()
    for d in range(1, NR):
        pl.semaphore_signal(barrier, inc=1, device_id=((r + d) % NR, k), device_id_type=MESH)
    for d in range(1, NK):
        pl.semaphore_signal(barrier, inc=1, device_id=(r, (k + d) % NK), device_id_type=MESH)

    loads = {}

    def load(name, src, dst):
        loads[name] = pltpu.make_async_copy(src, dst, ld.at[len(loads)])
        loads[name].start()

    pltpu.make_async_copy(resid.at[rows_of(r, ROWS), :], tok.at[:, rows_of(r, COLS)], tokR).start()
    load("g3", gw.at[:, pl.ds(384, 128)], gp.at[0])
    load("g10", gw.at[:, pl.ds(1280, 128)], gp.at[1])
    load("u3", uw.at[:, pl.ds(384, 128)], up.at[0])
    load("u10", uw.at[:, pl.ds(1280, 128)], up.at[1])
    load("gain2", gain2_h, gain2)
    load("gain1", gain1_h, gain1)
    load("lens", lens_h, lens)
    load("pos", pos_h, pos)

    pl.semaphore_wait(barrier, NR - 1 + NK - 1)

    load("wq", wq, wq_v)
    load("wk", wk, wk_v)
    load("wv", wv, wv_v)
    for d in range(1, NR):
        to = (r + d) % NR
        rc(resid.at[rows_of(to, ROWS), :], tok.at[:, rows_of(r, COLS)], tokS, tokR, (to, k)).start()
    for d in range(1, NK):
        pl.semaphore_signal(b2, inc=1, device_id=(r, (k + d) % NK), device_id_type=MESH)

    load("kc", kc, k_v)

    def w_copies(d):
        to = (l + d) % 4
        off = pl.multiple_of(piece_offset(to), 128)
        here = rows_of(l, COLS)
        pieces = (
            (gw.at[:, pl.ds(off, 384)], wp.at[c, here, pl.ds(0, 384)]),
            (uw.at[:, pl.ds(off, 384)], wp.at[c, here, pl.ds(384, 384)]),
            (pk.at[to], wp.at[c, here, pl.ds(768, 128)]),
        )
        if d == 0:
            return [pltpu.make_async_copy(s, t, wR) for s, t in pieces]
        return [rc(s, t, wS, wR, dev(to, m)) for s, t in pieces]

    def d_copies(d):
        to = (l + d) % 4
        off = pl.multiple_of(piece_offset(to), 64)
        off2 = pl.multiple_of(384 + 896 * (to // 2) + 64 * (to % 2), 64)
        here = rows_of(l, COLS)
        pieces = (
            (dw.at[pl.ds(off, 384), :], dwp.at[c, pl.ds(0, 384), here]),
            (dw.at[pl.ds(off2, 64), :], dwp.at[c, pl.ds(384, 64), here]),
        )
        if d == 0:
            return [pltpu.make_async_copy(s, t, dR) for s, t in pieces]
        return [rc(s, t, dS, dR, dev(to, m)) for s, t in pieces]

    w_sends = {d: w_copies(d) for d in range(4)}
    for d in (2, 1, 3, 0):
        w_sends[d][0].start()
        w_sends[d][1].start()
    for name in ("g3", "g10", "u3", "u10"):
        loads[name].wait()
    low = lax.broadcasted_iota(jnp.int32, (COLS, 128), 1) < 64
    for t in range(2):
        g = gp[t].astype(F32)
        u = up[t].astype(F32)
        pk[2 * t] = jnp.where(low, g, pltpu.roll(u, 64, 1)).astype(BF)
        pk[2 * t + 1] = jnp.where(low, pltpu.roll(g, 64, 1), u).astype(BF)
    for d in (1, 3, 2, 0):
        w_sends[d][2].start()
    def gain_copies():
        out = []
        for j in range(2):
            lj, mj = places(j)
            for d in range(1, 4):
                to = devj(j, (lj + d) % 4, mj)
                out.append(rc(gain2, gl.at[j, lj], gS.at[j, d - 1], gR.at[j, lj], to))
        return out

    load("vc", vc, v_v)
    loads["gain2"].wait()
    for j in range(2):
        gl[j, places(j)[0]] = gain2[...]
    for copy in gain_copies():
        copy.start()

    q3[...] = jnp.zeros_like(q3)
    k3[...] = jnp.zeros_like(k3)
    v3[...] = jnp.zeros_like(v3)
    for j in range(2):
        dwp[j, 448:512, :] = jnp.zeros((64, 1024), BF)

    load("wo", wo, wo_v)
    load("res", resid.at[rows_of(k, 64), :], res_v)

    loads["pos"].wait()
    loads["lens"].wait()
    loads["gain1"].wait()
    sub = lax.broadcasted_iota(jnp.int32, (8, 128), 0)
    lane = lax.broadcasted_iota(jnp.int32, (ROWS, HD), 1)
    p8 = jnp.broadcast_to(pos[...].astype(F32), (8, ROWS))
    place = lax.dot_general(
        p8, (sub == 0).astype(F32), TN, preferred_element_type=F32, precision=lax.Precision.HIGHEST
    )
    freq = jnp.exp((lane % 64).astype(F32) * (-2.0 * math.log(THETA) / HD))
    angle = place * freq
    cs = jnp.cos(angle)
    sn = jnp.where(lane < 64, -1.0, 1.0) * jnp.sin(angle)

    arrived(tok, tokR)
    t = tok[...].astype(F32)
    scale = 1.0 / jnp.sqrt(jnp.sum(t * t, axis=-1, keepdims=True) / MODEL_WIDTH + EPS)
    nrm[...] = (t * scale * gain1[...]).astype(BF)
    loads["wq"].wait()
    loads["wk"].wait()
    loads["wv"].wait()
    q = dot(nrm[...], wq_v[...])
    kn = dot(nrm[...], wk_v[...])
    vn = dot(nrm[...], wv_v[...])

    def rotate(v):
        return (v * cs + pltpu.roll(v, 64, 1) * sn).astype(BF).astype(F32)

    kn = rotate(kn)
    vn = vn.astype(BF).astype(F32)
    for h in range(HEADS):
        q3[pl.ds(h, ROWS, stride=8), :] = rotate(q[:, HD * h : HD * (h + 1)])
        k3[pl.ds(h, ROWS, stride=8), :] = kn
        v3[pl.ds(h, ROWS, stride=8), :] = vn

    factor = 1.0 / math.sqrt(HD)
    slot = lax.broadcasted_iota(jnp.int32, (8, SLOTS), 1)
    loads["kc"].wait()
    kd = r // 2
    for half in range(2):
        for b in range(16 * half, 16 * half + 16):
            rows = slice(8 * b, 8 * b + 8)
            s = lax.dot_general(q3[rows, :].astype(BF), k_v[b], NT, preferred_element_type=F32)
            n = lens[0, b]
            ok = (slot < n) & ((slot < SINKS) | (slot > n - WINDOW))
            s3[rows, :] = jnp.where(ok, s * factor, -1e30)
        rows = slice(128 * half, 128 * half + 128)
        s = s3[rows, :]
        own = jnp.sum(q3[rows, :] * k3[rows, :], axis=-1, keepdims=True) * factor
        peak = jnp.maximum(jnp.max(s, axis=-1, keepdims=True), own)
        e = jnp.where(s > -1e29, jnp.exp(s - peak), 0.0)
        eo = jnp.exp(own - peak)
        inv = 1.0 / (jnp.sum(e, axis=-1, keepdims=True) + eo)
        w3[rows, :] = e * inv
        o3[rows, :] = (eo * inv).astype(BF).astype(F32) * v3[rows, :]
        if half == 0:
            loads["vc"].wait()
        for b in range(16 * half, 16 * half + 16):
            rows = slice(8 * b, 8 * b + 8)
            o3[rows, :] += dot(w3[rows, :].astype(BF), v_v[b])
        ours = slice(16 * half, 16 * half + 16)
        for h in range(HEADS):
            att[ours, HD * h : HD * (h + 1)] = o3[pl.ds(128 * half + h, 16, stride=8), :].astype(BF)

        block = att.at[ours, :]
        there = attb.at[pl.ds(pl.multiple_of(ROWS * (r % 2) + 16 * half, 16), 16), rows_of(k, 512)]
        if half == 0:
            pl.semaphore_wait(b2, NK - 1)

        @pl.when(k == kd)
        def _():
            pltpu.make_async_copy(block, there, attR.at[k]).start()

        @pl.when(k != kd)
        def _():
            rc(block, there, attS, attR.at[k], (r, kd)).start()

        for d in range(1, NR):
            rc(block, there, attS, attR.at[k], ((r + d) % NR, kd)).start()

    loads["wo"].wait()
    loads["res"].wait()
    o = res_v[...].astype(F32)
    for d in (0, 1, 2, 3, 6, 7, 4, 5):
        kp = 2 * ((y + d // 2) % 4) + (c + d % 2) % 2
        arrived(attb.at[:, rows_of(kp, 512)], attR.at[kp])
        o = o + dot(attb[:, rows_of(kp, 512)], wo_v[rows_of(kp, 512), :])
    mid[...] = o
    mine = rows_of(y, 64)
    mb[mine, :] = (o * gain2[...]).astype(BF)

    around = (2, 1, 3)
    sets = (c, 1 - c)

    def line_sends(j, yp):
        lj, mj = places(j)
        at = rows_of(yp, 64)
        for e in around:
            rc(mb.at[at, :], al.at[j, at, rows_of(lj, COLS)], lS, alR.at[j, lj], devj(j, (lj + e) % 4, mj)).start()

    for e in around:
        rc(mb.at[mine, :], mb.at[mine, :], yS, yR.at[y], (r, 2 * ((y + e) % 4) + c)).start()
    for j in sets:
        line_sends(j, y)
    for i, j in enumerate(sets):
        for e in around:
            yp = (y + e) % 4
            if i == 0:
                arrived(mb.at[rows_of(yp, 64), :], yR.at[yp])
            line_sends(j, yp)
    arrived(wp.at[c], wR)
    rc(wp.at[c], wp.at[c], swS, swR, sibling).start()
    for d in (1, 3, 2, 0):
        for copy in d_copies(d):
            copy.start()
    for j in range(2):
        al[j, :, rows_of(places(j)[0], COLS)] = mb[...]

    @pl.when(k == kd)
    def _():
        arrived(attb.at[pl.ds(0, 32), pl.ds(0, 3584)], attS)
        arrived(attb.at[pl.ds(32, 32), pl.ds(0, 4096)], attS)

    @pl.when(k != kd)
    def _():
        arrived(attb, attS)

    def silu(v):
        return v / (1.0 + jnp.exp(-v))

    def gate(j):
        lj, mj = places(j)
        for e in around:
            lp = (lj + e) % 4
            arrived(al.at[j, :, rows_of(lp, COLS)], alR.at[j, lp])
        pb[j] = dot(al[j], wp[j]).astype(BF)
        for e in around:
            mi = (mj + e) % 4
            rc(pb.at[j, rows_of(mi, 64), :], rf.at[j, mj], rfS, rfR.at[j, mj], devj(j, lj, mi)).start()
        for e in around:
            at = (lj + e) % 4
            arrived(gl.at[j, at], gR.at[j, at])
        part = jnp.zeros((256, 128), F32)
        for i in range(8):
            g = 1.0 / gl[j, i // 2, :, 128 * (i % 2) : 128 * (i % 2) + 128]
            v = al[j, :, 128 * i : 128 * (i + 1)].astype(F32) * g
            part = part + v * v
        sqm[j, mj] = lax.dot_general(
            jnp.ones((8, 128), F32), part, NT, preferred_element_type=F32, precision=lax.Precision.HIGHEST
        )
        for e in around:
            mi = (mj + e) % 4
            rc(sqm.at[j, mj], sqm.at[j, mj], sqS, sqR.at[j, mj], devj(j, lj, mi)).start()

    def hide(j):
        lj, mj = places(j)
        here = rows_of(mj, 64)
        for e in around:
            mi = (mj + e) % 4
            arrived(sqm.at[j, mi], sqR.at[j, mi])
        total = lax.dot_general(
            sqm[j, 0] + sqm[j, 1] + sqm[j, 2] + sqm[j, 3],
            (sub == 0).astype(F32),
            TN,
            preferred_element_type=F32,
            precision=lax.Precision.HIGHEST,
        )
        invs[...] = 1.0 / jnp.sqrt(total / MODEL_WIDTH + EPS)
        inv = invs[here, :]
        for e in around:
            mi = (mj + e) % 4
            arrived(rf.at[j, mi], rfR.at[j, mi])

        def tile(i):
            at = slice(128 * i, 128 * (i + 1))
            v = pb[j, here, at].astype(F32)
            for e in around:
                v = v + rf[j, (mj + e) % 4, :, at].astype(F32)
            return v * inv

        for i in range(3):
            hb[j, here, 128 * i : 128 * (i + 1)] = (silu(tile(i)) * tile(3 + i)).astype(BF)
        t = tile(6)
        low = lax.broadcasted_iota(jnp.int32, (64, 128), 1) < 64
        hb[j, here, 384:512] = jnp.where(low, silu(t) * pltpu.roll(t, 64, 1), 0.0).astype(BF)
        for e in around:
            rc(hb.at[j, here, :], hb.at[j, here, :], hS, hR.at[j, mj], devj(j, lj, (mj + e) % 4)).start()

    gate(c)
    arrived(wp.at[1 - c], swR)
    gate(1 - c)
    for j in sets:
        hide(j)
    arrived(dwp.at[c, pl.ds(0, 448), :], dR)
    rc(dwp.at[c, pl.ds(0, 448), :], dwp.at[c, pl.ds(0, 448), :], sdS, sdR, sibling).start()

    arrived(tok.at[:, pl.ds(0, COLS * 15)], tokS)
    arrived(wp.at[c, pl.ds(0, 768), :], wS)
    for copy in gain_copies():
        copy.wait_send()
    arrived(wp.at[c], swS)
    arrived(mb.at[pl.ds(0, 192), :], yS)
    arrived(al.at[:, :, pl.ds(0, 768)], lS)
    arrived(pb.at[:, pl.ds(0, 192), :], rfS)
    arrived(sqm.at[:, pl.ds(0, 3)], sqS)
    arrived(dwp.at[c, pl.ds(0, 448), pl.ds(0, 768)], dS)

    def down(j):
        lj, mj = places(j)
        for e in around:
            mi = (mj + e) % 4
            arrived(hb.at[j, rows_of(mi, 64), :], hR.at[j, mi])
        yb[j] = dot(hb[j], dwp[j]).astype(BF)
        for e in around:
            to = (lj + e) % 4
            rc(yb.at[j, :, rows_of(to, COLS)], yr.at[j, lj], oS, oR.at[j, lj], devj(j, to, mj)).start()

    down(c)
    arrived(dwp.at[1 - c, pl.ds(0, 448), :], sdR)
    down(1 - c)
    v = jnp.zeros((256, COLS), F32)
    for j in sets:
        lj, mj = places(j)
        v = v + yb[j, :, rows_of(lj, COLS)].astype(F32)
        for e in around:
            lp = (lj + e) % 4
            arrived(yr.at[j, lp], oR.at[j, lp])
            v = v + yr[j, lp].astype(F32)
    vf[...] = v
    fs[...] = v.astype(BF)
    for e in around:
        yp = (y + e) % 4
        rc(fs.at[rows_of(yp, 64), :], fb.at[y], fS, fR.at[y], (r, 2 * yp + c)).start()
    arrived(hb.at[:, pl.ds(0, 192), :], hS)
    arrived(yb.at[:, :, pl.ds(0, 768)], oS)
    arrived(dwp.at[c, pl.ds(0, 448), :], sdS)
    res = mid[...] + vf[mine, :]
    for e in around:
        yp = (y + e) % 4
        arrived(fb.at[yp], fR.at[yp])
        res = res + fb[yp].astype(F32)
    out[...] = res.astype(BF)
    arrived(fs.at[pl.ds(0, 192), :], fS)


def shards(
    residual_in,
    attn_gain,
    query_weight,
    key_matrix,
    value_matrix,
    key_cache,
    cached_values,
    cache_lengths,
    positions,
    output_weight,
    mlp_gain,
    gate_weight,
    up_weight,
    down_weight,
):
    hbm = pl.BlockSpec(memory_space=pltpu.MemorySpace.HBM)
    vmem = pl.BlockSpec(memory_space=pltpu.MemorySpace.VMEM)
    V = pltpu.VMEM
    dma = lambda *shape: pltpu.SemaphoreType.DMA(shape) if shape else pltpu.SemaphoreType.DMA
    return pl.pallas_call(
        kernel,
        out_shape=jax.ShapeDtypeStruct((64, COLS), BF),
        in_specs=[hbm] * 14,
        out_specs=vmem,
        scratch_shapes=[
            pltpu.SMEM((1, ROWS), jnp.int32),
            V((1, ROWS), jnp.int32),
            V((1, MODEL_WIDTH), F32),
            V((1, COLS), F32),
            V((ROWS, MODEL_WIDTH), BF),
            V((ROWS, MODEL_WIDTH), BF),
            V((MODEL_WIDTH, HEADS * HD), BF),
            V((MODEL_WIDTH, HD), BF),
            V((MODEL_WIDTH, HD), BF),
            V((ROWS, SLOTS, HD), BF),
            V((ROWS, SLOTS, HD), BF),
            V((8 * ROWS, HD), F32),
            V((8 * ROWS, HD), F32),
            V((8 * ROWS, HD), F32),
            V((8 * ROWS, HD), F32),
            V((8 * ROWS, SLOTS), F32),
            V((8 * ROWS, SLOTS), F32),
            V((ROWS, HEADS * HD), BF),
            V((64, MODEL_WIDTH), BF),
            V((MODEL_WIDTH, COLS), BF),
            V((64, COLS), BF),
            V((2, COLS, 128), BF),
            V((2, COLS, 128), BF),
            V((4, COLS, 128), BF),
            V((2, 1024, CHUNK), BF),
            V((2, 512, 1024), BF),
            V((2, 4, 1, COLS), F32),
            V((2, 256, 1024), BF),
            V((64, COLS), F32),
            V((2, 256, CHUNK), BF),
            V((2, 4, 64, CHUNK), BF),
            V((2, 256, 512), BF),
            V((2, 256, 1024), BF),
            V((2, 4, 256, COLS), BF),
            V((256, COLS), F32),
            V((256, COLS), BF),
            V((4, 64, COLS), BF),
            V((256, 128), F32),
            V((2, 4, 8, 256), F32),
            V((256, COLS), BF),
            dma(15),
            dma(),
            dma(),
            dma(),
            dma(),
            dma(),
            dma(),
            dma(2, 3),
            dma(2, 4),
            dma(),
            dma(NK),
            pltpu.SemaphoreType.REGULAR,
            dma(),
            dma(4),
            dma(),
            dma(2, 4),
            dma(),
            dma(2, 4),
            dma(),
            dma(2, 4),
            dma(),
            dma(2, 4),
            dma(),
            dma(2, 4),
            dma(),
            dma(4),
            dma(),
            dma(),
            dma(),
            dma(),
        ],
        compiler_params=pltpu.CompilerParams(
            collective_id=0, has_side_effects=True, vmem_limit_bytes=56 << 20
        ),
    )(
        cache_lengths.reshape(1, ROWS),
        positions.reshape(1, ROWS),
        residual_in,
        attn_gain.reshape(1, MODEL_WIDTH),
        query_weight,
        key_matrix,
        value_matrix,
        key_cache.reshape(ROWS, SLOTS, HD),
        cached_values.reshape(ROWS, SLOTS, HD),
        output_weight,
        mlp_gain.reshape(1, COLS),
        gate_weight,
        up_weight,
        down_weight,
    )


def solution(mesh):
    return jax.shard_map(
        shards,
        mesh=mesh,
        in_specs=(
            P(None, "req"),
            P(),
            P(None, "kv"),
            P(None, "kv"),
            P(None, "kv"),
            P("req", "kv", None, None),
            P("req", "kv", None, None),
            P("req"),
            P("req"),
            P(None, "req"),
            P("req"),
            P("req", "kv"),
            P("req", "kv"),
            P("kv", "req"),
        ),
        out_specs=P("kv", "req"),
        check_vma=False,
    )
```
